128 devices in a mesh: grp: 4 (over y), fsdp: 32 (over x, z, core).
Axes of the slice: x: 4, y: 4, z: 4, core: 2. Of those that a mesh axis runs over, the one named last changes fastest.
Arguments:
- hidden: bfloat16 [256, 257, 1024], P(('grp', 'fsdp')), may hold values from -6 to 6
- ln1_gain: float32 [1024], replicated, may hold values from 0.25 to 1.75
- w_qkv: bfloat16 [1024, 3072], P('fsdp'), may hold values from -0.1875 to 0.1875
- w_out: bfloat16 [1024, 1024], P('fsdp'), may hold values from -0.1875 to 0.1875
- ln2_gain: float32 [1024], replicated, may hold values from 0.25 to 1.75
- w_up: bfloat16 [1024, 4096], P('fsdp'), may hold values from -0.1875 to 0.1875
- w_down: bfloat16 [4096, 1024], P('fsdp'), may hold values from -0.09375 to 0.09375
- post_gain: float32 [1024], replicated, may hold values from 0.25 to 1.75
- w_proj: bfloat16 [1024, 256], replicated, may hold values from -0.1875 to 0.1875
- table: float32 [128, 2048, 256], P(('grp', 'fsdp')), may hold values from -6 to 6
- accum: float32 [128, 2048, 256], P(('grp', 'fsdp')), may hold values from 0.1 to 4
- place: int32 [128], replicated, may hold values from 0 to 127, each once
- lookup_table: int32 [16384, 1], P(('grp', 'fsdp')), may hold values from 0 to 127; in each aligned block of 128 rows (0 to 127, 128 to 255, ...) at most 2 rows name the same one
- lookup_row: int32 [16384], P(('grp', 'fsdp')), may hold values from 0 to 2047
Outputs:
- table_new: float32 [128, 2048, 256], P(('grp', 'fsdp'))
- accum_new: float32 [128, 2048, 256], P(('grp', 'fsdp'))
- content_grad: float32 [256, 256], P(('grp', 'fsdp'))
- proj_grad: float32 [1024, 256], P(('grp', 'fsdp'))
The draws below stay inside these ranges and needn't reach their ends.
Inputs may be any that keep to these rules, and one draw needn't show every extreme that they name: `lookup_table`: within the lookups of one device (aligned blocks of 128), no table is named more than 2 times, a bound that some block reaches. `place`: every device holds exactly one table.
All inputs are finite; a program needn't handle non-finite values.
Results may differ from the reference program's by a relative error of at most 0.0044.
Values may be sent and summed in bfloat16 or wider, within the bound.
A program may use at most 192 MiB of HBM per device.

```python
import math
import jax
import jax.numpy as jnp
import numpy as np
from jax import lax

D = 1024
HEADS = 16
MLP = 4096
SEQ = 257
PROJ = 256
LOOK_IMG = 64
ROWS_DEV = 2048
LOOK_DEV = 128
TABLES = 128
CAP = 2
IMAGES = 256
LOOKUPS = 16384
DEVICES = 128


def place_ends(entries, rng, low, top_value):
    spot = [jax.random.randint(jax.random.fold_in(rng, axis), (), 0, length) for axis, length in enumerate(entries.shape)]
    main_axis = entries.shape.index(max(entries.shape))
    neighbour = spot[:main_axis] + [(spot[main_axis] + 1) % entries.shape[main_axis]] + spot[main_axis + 1:]
    return entries.at[tuple(spot)].set(low).at[tuple(neighbour)].set(top_value)


def steps_of(rng, shape, pieces, smallest, high):
    level, own = 1.0, jax.random.fold_in(rng, 6)
    for axis_at, blocks in pieces:
        heights = jnp.exp(jax.random.uniform(jax.random.fold_in(own, axis_at), (blocks,), jnp.float32, smallest / len(pieces), high / len(pieces)))
        level = level * jnp.repeat(heights, shape[axis_at] // blocks).reshape([-1 if axis == axis_at else 1 for axis in range(len(shape))])
    return level


def deal_out(stream_key, own, number, rows, number_of, top, reach, skew):
    sequence = jax.random.permutation(stream_key, number_of)
    heavy_load, usual = portions_of(number_of, rows * top, reach, skew, True), portions_of(number_of, rows * top, reach, skew, False)
    places = jnp.arange(number_of)

    def named(sizes, turn):
        used = int((sizes > 0).sum())
        fixed = max(1, used // 4)
        moved = fixed + (places - fixed + turn * (used - fixed)) % max(1, number_of - fixed)
        return jnp.zeros((number_of,), jnp.int32).at[sequence[jnp.where(places < fixed, places, moved)]].set(jnp.asarray(sizes, jnp.int32))

    sizes = jnp.where(number % 4 == 0, named(heavy_load, number // 4), named(usual, number - number // 4 - 1))
    mixed = jax.random.permutation(jax.random.fold_in(own, 3), number_of)
    source_of, taker = mixed[0:number_of // 2 * 2:2], mixed[1:number_of // 2 * 2:2]
    margin = jnp.minimum(sizes[source_of] - 1, reach - sizes[taker]) // 2
    margin = jnp.where((source_of == sequence[0]) | (taker == sequence[0]) | (sizes[taker] == 0), 0, jnp.maximum(margin, 0))
    moved = jax.random.randint(jax.random.fold_in(own, 4), (number_of // 2,), 0, 1 << 20) % (margin + 1)
    sizes = sizes.at[source_of].add(-moved).at[taker].add(moved)
    labels = jnp.searchsorted(jnp.cumsum(sizes), jnp.arange(rows * top), side="right").astype(jnp.int32)
    listing = labels.reshape(top, rows).T
    listing = listing[jax.random.permutation(jax.random.fold_in(own, 1), rows)]
    turn = jax.random.randint(jax.random.fold_in(own, 2), (rows, 1), 0, top)
    return jnp.take_along_axis(listing, (jnp.arange(top)[None, :] + turn) % top, axis=1)


def portions_of(count, total, bound, slope, full):
    weights = [(1 << 20) // math.isqrt(standing ** slope) + 1 for standing in range(1, count + 1)]
    largest = bound if full else min(bound, max(-(-total // count), total * weights[0] // sum(weights)))
    least = 1 if total - largest >= count - 1 else 0
    given, spare = [largest] + [least] * (count - 1), total - largest - least * (count - 1)
    while spare > 0:
        candidates = [i for i in range(1, count) if given[i] < largest] or [i for i in range(1, count) if given[i] < bound]
        pool, budget = sum([weights[i] for i in candidates]), spare
        for i in candidates:
            extra = min(bound - given[i], max(1, budget * weights[i] // pool), spare)
            given[i] = given[i] + extra
            spare = spare - extra
    return np.array(given)


def bell_draw(own_key, dims, deviation, reach, pieces=(), kind=jnp.bfloat16):
    result = jax.random.normal(own_key, dims, jnp.float32) * deviation
    if len(pieces) > 0:
        result = steps_of(own_key, dims, pieces, -0.22, 0.18) * result
    return jnp.clip(result, min=-reach, max=reach).astype(kind)


def setup_inputs(seed: int = 0) -> dict:
    streams_of = jax.random.split(jax.random.key(seed), 15)
    hidden = bell_draw(streams_of[0], (IMAGES, SEQ, D), 1.0, 6.0, ((0, 128),))
    ln1_gain = jnp.clip(1.0 + 0.15 * jax.random.normal(streams_of[1], (D,), jnp.float32), 0.25, 1.75)
    w_qkv = bell_draw(streams_of[2], (D, 3 * D), D ** -0.5, 0.1875, ((0, 32),))
    w_out = bell_draw(streams_of[3], (D, D), D ** -0.5, 0.1875, ((0, 32),))
    ln2_gain = jnp.clip(1.0 + 0.15 * jax.random.normal(streams_of[4], (D,), jnp.float32), 0.25, 1.75)
    w_up = bell_draw(streams_of[5], (D, MLP), D ** -0.5, 0.1875, ((0, 32),))
    w_down = bell_draw(streams_of[6], (MLP, D), MLP ** -0.5, 0.09375, ((0, 32),))
    post_gain = jnp.clip(1.0 + 0.15 * jax.random.normal(streams_of[7], (D,), jnp.float32), 0.25, 1.75)
    w_proj = bell_draw(streams_of[8], (D, PROJ), D ** -0.5, 0.1875)
    table = bell_draw(streams_of[9], (DEVICES, ROWS_DEV, PROJ), 1.0, 6.0, ((0, 128),), jnp.float32)
    accum = jnp.clip(jnp.exp(math.log(4.0) - 3.6888794 * jax.random.uniform(streams_of[10], (DEVICES, ROWS_DEV, PROJ), jnp.float32) ** steps_of(streams_of[10], (DEVICES, ROWS_DEV, PROJ), ((0, 128),), -0.2, 0.2)), 0.1, 4.0)
    place = jax.random.permutation(streams_of[11], TABLES).astype(jnp.int32)
    lookup_table_keys = jax.random.split(jax.random.fold_in(streams_of[12], 1), LOOKUPS // LOOK_DEV)
    lookup_table_turns = jax.random.permutation(jax.random.fold_in(streams_of[12], 3), LOOKUPS // LOOK_DEV)
    lookup_table = jax.vmap(lambda own, number: deal_out(jax.random.fold_in(streams_of[12], 2), own, number, LOOK_DEV, TABLES, 1, CAP, 2))(lookup_table_keys, lookup_table_turns).reshape((LOOKUPS, 1))
    lookup_row = place_ends(jax.random.randint(streams_of[13], (LOOKUPS,), 0, ROWS_DEV), jax.random.fold_in(streams_of[13], 1), 0, ROWS_DEV - 1).astype(jnp.int32)
    return {"hidden": hidden, "ln1_gain": ln1_gain, "w_qkv": w_qkv, "w_out": w_out, "ln2_gain": ln2_gain, "w_up": w_up, "w_down": w_down, "post_gain": post_gain, "w_proj": w_proj, "table": table, "accum": accum, "place": place, "lookup_table": lookup_table, "lookup_row": lookup_row}


epsilon = 1e-06
learn_rate = 0.5

def layer_norm(values, gain):
    center = lax.optimization_barrier(jnp.mean(values, axis=-1, keepdims=True))
    shifted = values - center
    spread = lax.optimization_barrier(jnp.mean(shifted * shifted, axis=-1, keepdims=True))
    return shifted * lax.rsqrt(spread + epsilon) * gain.astype(jnp.float32)

def encode_block(block, ln1_gain, w_qkv, w_out, ln2_gain, w_up, w_down, post_gain):
    images, seq, width = block.shape
    head_dim = width // HEADS
    tokens = block.reshape(images * seq, width)
    normed = layer_norm(tokens.astype(jnp.float32), ln1_gain).astype(jnp.bfloat16)
    qkv = jnp.dot(normed, w_qkv, preferred_element_type=jnp.float32).astype(jnp.bfloat16)
    qkv = qkv.reshape(images, seq, 3, HEADS, head_dim)
    query = qkv[:, :, 0].astype(jnp.float32)
    keys = qkv[:, :, 1].astype(jnp.float32)
    values = qkv[:, :, 2].astype(jnp.float32)
    scores = jnp.einsum('bqhd,bkhd->bhqk', query, keys) / math.sqrt(head_dim)
    probs = jax.nn.softmax(scores, axis=-1).astype(jnp.bfloat16)
    mixed = jnp.einsum('bhqk,bkhd->bqhd', probs.astype(jnp.float32), values)
    mixed = mixed.astype(jnp.bfloat16).reshape(images * seq, width)
    resid = tokens.astype(jnp.float32) + jnp.dot(mixed, w_out, preferred_element_type=jnp.float32)
    resid = resid.astype(jnp.bfloat16)
    normed_two = layer_norm(resid.astype(jnp.float32), ln2_gain).astype(jnp.bfloat16)
    upward = jnp.dot(normed_two, w_up, preferred_element_type=jnp.float32)
    active = jax.nn.gelu(upward, approximate=False).astype(jnp.bfloat16)
    final = resid.astype(jnp.float32) + jnp.dot(active, w_down, preferred_element_type=jnp.float32)
    posted = layer_norm(final, post_gain).reshape(images, seq, width)
    return lax.optimization_barrier(jnp.mean(posted, axis=1)).astype(jnp.bfloat16)

def reference(hidden, ln1_gain, w_qkv, w_out, ln2_gain, w_up, w_down, post_gain, w_proj, table, accum, place, lookup_table, lookup_row):
    blocks = hidden.reshape(-1, 8, SEQ, D)

    def encode_one(block):
        return encode_block(block, ln1_gain, w_qkv, w_out, ln2_gain, w_up, w_down, post_gain)
    pooled = lax.map(encode_one, blocks).reshape(-1, D)
    content = jnp.dot(pooled, w_proj, preferred_element_type=jnp.float32)
    scale = lax.rsqrt(lax.optimization_barrier(jnp.mean(content * content, axis=-1, keepdims=True)) + epsilon)
    unit = content * scale
    owner = place[lookup_table[:, 0]].astype(jnp.int32)
    flat = (owner * ROWS_DEV + lookup_row).astype(jnp.int32)
    flat_table = table.reshape(-1, PROJ)
    diff = flat_table[flat] - jnp.repeat(unit, LOOK_IMG, axis=0)
    grad_rows = jnp.zeros(flat_table.shape, jnp.float32).at[flat].add(diff)
    accum_new = accum.reshape(-1, PROJ) + grad_rows * grad_rows
    table_new = flat_table - learn_rate * grad_rows / jnp.sqrt(accum_new)
    grad_unit = -lax.optimization_barrier(jnp.sum(diff.reshape(-1, LOOK_IMG, PROJ), axis=1))
    inner = lax.optimization_barrier(jnp.mean(grad_unit * unit, axis=-1, keepdims=True))
    content_grad = scale * (grad_unit - unit * inner)
    proj_grad = jnp.dot(pooled.astype(jnp.float32).T, content_grad, precision=lax.Precision.HIGHEST, preferred_element_type=jnp.float32)
    return (table_new.reshape(table.shape), accum_new.reshape(accum.shape), content_grad, proj_grad)
```

```python
import math

import jax
import jax.numpy as jnp
from jax import lax
from jax.sharding import Mesh
from jax.sharding import PartitionSpec as P

HEADS = 16
LOOK_IMG = 64
FSDP = ("fsdp_0", "fsdp_1", "fsdp_2")
GRP_FSDP = ("grp", "fsdp_0", "fsdp_1", "fsdp_2")


epsilon = 1e-06
learn_rate = 0.5


def sent_together(arrays, axis, dim, along):
    widths = [a.shape[along] for a in arrays]
    both = jnp.concatenate(arrays, axis=along)
    out = lax.all_gather(both, axis, axis=dim, tiled=True)
    return tuple(jnp.split(out, [sum(widths[:k]) for k in range(1, len(widths))], axis=along))


def in_blocks(array, dim, devices):
    shape = array.shape
    tiles = array.reshape(*shape[:dim], devices, shape[dim] // devices, *shape[dim + 1 :])
    return jnp.moveaxis(tiles, dim, 0)


def laid_out(tiles, dim):
    tiles = jnp.moveaxis(tiles, 0, dim)
    shape = tiles.shape
    return tiles.reshape(*shape[:dim], shape[dim] * shape[dim + 1], *shape[dim + 2 :])


def turned_blocks(tiles, axes, sequence):
    shape = [lax.axis_size(a) for a in axes]
    tiles = tiles.reshape(*shape, *tiles.shape[1:])
    for k in sequence:
        tiles = lax.all_to_all(tiles, axes[k], split_axis=k, concat_axis=k, tiled=True)
    return tiles.reshape(-1, *tiles.shape[len(axes) :])


def core_and_chips(array, groups, sequence, split_dim, concat_dim):
    devices = lax.axis_size(groups[0]) * lax.axis_size(groups[1])
    tiles = in_blocks(array, split_dim, devices)
    return laid_out(turned_blocks(tiles, groups, sequence), concat_dim)


def layer_norm(values, gain):
    center = jnp.mean(values, axis=-1, keepdims=True)
    shifted = values - center
    spread = jnp.mean(shifted * shifted, axis=-1, keepdims=True)
    return shifted * lax.rsqrt(spread + epsilon) * gain


def attend(qkv, images, seq, width):
    head_dim = width // HEADS
    parts = qkv.reshape(images, seq, 3, HEADS, head_dim)
    scores = jnp.einsum(
        "bqhd,bkhd->bhqk", parts[:, :, 0], parts[:, :, 1], preferred_element_type=jnp.float32
    ) / math.sqrt(head_dim)
    probs = jax.nn.softmax(scores, axis=-1).astype(jnp.bfloat16)
    mixed = jnp.einsum("bhqk,bkhd->bqhd", probs, parts[:, :, 2], preferred_element_type=jnp.float32)
    return mixed.astype(jnp.bfloat16).reshape(images * seq, width)


def named_counts(lookup_table, lookup_row, place, images, rows_dev, me):
    table_ids = jnp.arange(place.shape[0], dtype=jnp.int32)
    owners = jnp.sum(jnp.where(lookup_table == table_ids[None, :], place[None, :], 0), axis=1)
    image = jnp.arange(lookup_row.shape[0], dtype=jnp.int32) // LOOK_IMG
    named = (owners * rows_dev + lookup_row) * images + image
    every = lax.all_gather(named[None, :], GRP_FSDP, axis=0, tiled=True)
    code = every - me * (rows_dev * images)
    mine = (code >= 0) & (code < rows_dev * images)
    first = jnp.max(jnp.where(mine, code, -1), axis=1)
    second = jnp.min(jnp.where(mine, code, rows_dev * images), axis=1)
    second = jnp.where(jnp.sum(mine.astype(jnp.int32), axis=1) > 1, second, -1)
    wanted = jnp.arange(rows_dev, dtype=jnp.int32)[:, None] * images + (
        jnp.arange(every.shape[0] * images, dtype=jnp.int32) % images
    )[None, :]
    hit = lambda codes: (wanted == jnp.repeat(codes, images)[None, :]).astype(jnp.float32)
    return hit(first) + hit(second)


def on_device(
    hidden,
    ln1_gain,
    w_qkv,
    w_out,
    ln2_gain,
    w_up,
    w_down,
    post_gain,
    w_proj,
    table,
    accum,
    place,
    lookup_table,
    lookup_row,
):
    images, seq, width = hidden.shape
    count = images * seq
    tokens = hidden.reshape(count, width)
    n_devices = lax.axis_size(GRP_FSDP)
    me = lax.axis_index(GRP_FSDP)
    local_table = table[0]
    rows_dev = local_table.shape[0]
    counts = named_counts(lookup_table, lookup_row, place, images, rows_dev, me)
    row_sums = lax.psum(
        lax.dot_general(counts, local_table, (((0,), (0,)), ((), ())), precision=lax.Precision.HIGHEST, preferred_element_type=jnp.float32),
        GRP_FSDP,
    )
    full_qkv, full_out, full_up, full_down = (
        *sent_together((w_qkv, w_out, w_up), FSDP, 0, 1),
        lax.all_gather(w_down, FSDP, axis=0, tiled=True),
    )
    normed = layer_norm(tokens.astype(jnp.float32), ln1_gain).astype(jnp.bfloat16)
    qkv = jnp.dot(normed, full_qkv, preferred_element_type=jnp.float32)
    mixed = attend(qkv.astype(jnp.bfloat16), images, seq, width)
    projected = jnp.dot(mixed, full_out, preferred_element_type=jnp.float32)
    resid = (tokens.astype(jnp.float32) + projected).astype(jnp.bfloat16)
    normed_two = layer_norm(resid.astype(jnp.float32), ln2_gain).astype(jnp.bfloat16)
    upward = jnp.dot(normed_two, full_up, preferred_element_type=jnp.float32)
    active = jax.nn.gelu(upward, approximate=False).astype(jnp.bfloat16)
    downward = jnp.dot(active, full_down, preferred_element_type=jnp.float32)
    final = resid.astype(jnp.float32) + downward
    posted = layer_norm(final, post_gain).reshape(images, seq, width)
    pooled = jnp.mean(posted, axis=1).astype(jnp.bfloat16)
    content = jnp.dot(pooled, w_proj, preferred_element_type=jnp.float32)
    scale = lax.rsqrt(jnp.mean(content * content, axis=-1, keepdims=True) + epsilon)
    unit = content * scale
    del scale, unit
    everyone = lax.all_gather(pooled, GRP_FSDP, axis=0, tiled=True)
    content_all = jnp.dot(everyone, w_proj, preferred_element_type=jnp.float32)
    scale_all = lax.rsqrt(jnp.mean(content_all * content_all, axis=-1, keepdims=True) + epsilon)
    unit_all = content_all * scale_all
    grad_unit = LOOK_IMG * unit_all - row_sums
    inner = jnp.mean(grad_unit * unit_all, axis=-1, keepdims=True)
    grad_all = scale_all * (grad_unit - unit_all * inner)
    content_grad = lax.dynamic_slice_in_dim(grad_all, images * me, images, axis=0)
    share = width // n_devices
    columns = lax.dynamic_slice_in_dim(everyone, share * me, share, axis=1).astype(jnp.float32)
    proj_grad = jnp.dot(columns.T, grad_all, precision=lax.Precision.HIGHEST, preferred_element_type=jnp.float32)
    named = jnp.sum(counts, axis=1, keepdims=True)
    unit_sums = jnp.dot(counts, unit_all, precision=lax.Precision.HIGHEST, preferred_element_type=jnp.float32)
    grad_rows = named * local_table - unit_sums
    accum_new = accum[0] + grad_rows * grad_rows
    table_new = local_table - learn_rate * grad_rows / jnp.sqrt(accum_new)
    return (table_new[None], accum_new[None], content_grad, proj_grad)


def solution(mesh):
    torus = Mesh(
        mesh.devices.reshape(mesh.shape["grp"], 4, 4, 2), ("grp", "fsdp_0", "fsdp_1", "fsdp_2")
    )
    in_specs = (
        P(GRP_FSDP, None, None),
        P(),
        P(FSDP, None),
        P(FSDP, None),
        P(),
        P(FSDP, None),
        P(FSDP, None),
        P(),
        P(),
        P(GRP_FSDP, None, None),
        P(GRP_FSDP, None, None),
        P(),
        P(GRP_FSDP, None),
        P(GRP_FSDP),
    )
    out_specs = (
        P(GRP_FSDP, None, None),
        P(GRP_FSDP, None, None),
        P(GRP_FSDP, None),
        P(GRP_FSDP, None),
    )
    return jax.shard_map(
        on_device, mesh=torus, in_specs=in_specs, out_specs=out_specs, check_vma=False
    )
```

```python
import functools

import jax
import jax.numpy as jnp
from jax import lax
from jax.experimental import pallas as pl
from jax.experimental.pallas import tpu as pltpu
from jax.sharding import Mesh
from jax.sharding import PartitionSpec as P

HEADS = 16
LOOK_IMG = 64
FSDP = ("fsdp_0", "fsdp_1", "fsdp_2")
GRP_FSDP = ("grp", "fsdp_0", "fsdp_1", "fsdp_2")
MESH = pl.DeviceIdType.MESH
PAD = 272
BLK = 32

epsilon = 1e-06
learn_rate = 0.5


def here():
    return tuple(lax.axis_index(a) for a in GRP_FSDP)


def moved(pos, axis, step):
    out = list(pos)
    out[axis] = lax.rem(pos[axis] + step, 2 if axis == 3 else 4)
    return tuple(out)


def wait_bytes(ref, sem):
    pltpu.make_async_copy(ref, ref, sem).wait()


class Weights:
    def __init__(self, own, full, sems, pos):
        self.own, self.full, self.sems = own, full, sems
        y, x, z, c = pos
        self.rows = own.shape[0]
        self.partner = (y, x, z, 1 - c)
        d = 1 - c
        self.i, self.j, self.c = x * d + z * c, z * d + x * c, c
        self.s1, self.s2 = 8 - 6 * c, 2 + 6 * c
        self.first = {k: (y, lax.rem(x + k * d, 4), lax.rem(z + k * c, 4), c) for k in (1, 3)}
        self.second = {k: (y, lax.rem(x + k * c, 4), lax.rem(z + k * d, 4), c) for k in (1, 3)}

    def part(self, di, dj, lo=0, size=None):
        size = self.rows if size is None else size
        block = lax.rem(self.i + di, 4) * self.s1 + lax.rem(self.j + dj, 4) * self.s2 + self.c
        return self.full.at[pl.ds(pl.multiple_of(block * self.rows + lo, 16), size)]

    def send(self, ref, sem, device, src=None):
        pltpu.make_async_remote_copy(
            src_ref=ref if src is None else src,
            dst_ref=ref,
            send_sem=self.sems.at[0],
            recv_sem=self.sems.at[sem],
            device_id=device,
            device_id_type=MESH,
        ).start()

    def got(self, ref, sem):
        wait_bytes(ref, self.sems.at[sem])

    def to_partner(self, ref, src=None):
        self.send(ref, 1, self.partner, src)

    def step0(self):
        mine = self.part(0, 0)
        pltpu.make_async_copy(self.own, mine, self.sems.at[2]).start()
        self.send(mine, 3, self.first[1], self.own)
        self.send(mine, 4, self.first[3], self.own)
        self.send(mine, 7, self.second[1], self.own)
        self.send(mine, 11, self.second[3], self.own)
        self.to_partner(mine, self.own)

    def spread(self, di, k):
        block = self.part(di, 0)
        self.send(block, 7 + k, self.second[1])
        self.send(block, 11 + k, self.second[3])
        self.to_partner(block)

    def step1(self):
        half = self.rows // 2
        self.got(self.part(3, 0), 3)
        self.send(self.part(3, 0, 0, half), 5, self.first[1])
        self.got(self.part(1, 0), 4)
        self.send(self.part(1, 0, half, half), 6, self.first[3])
        self.spread(3, 1)
        self.spread(1, 2)

    def step2(self):
        half = self.rows // 2
        self.got(self.part(2, 0, 0, half), 5)
        self.got(self.part(2, 0, half, half), 6)
        self.spread(2, 3)

    def pass_on(self, k, di):
        before, after = self.part(di, 3), self.part(di, 1)
        self.got(before, 7 + k)
        if k in (0, 2):
            self.send(before, 15 + k // 2, self.second[1])
        self.to_partner(before)
        self.got(after, 11 + k)
        if k in (1, 3):
            self.send(after, 17 + k // 2, self.second[3])
        self.to_partner(after)

    def step3(self):
        self.pass_on(0, 0)
        self.pass_on(1, 3)

    def step4(self):
        self.pass_on(2, 1)
        self.pass_on(3, 2)

    def step5(self):
        for sem, di in ((15, 0), (16, 1), (17, 3), (18, 2)):
            block = self.part(di, 2)
            self.got(block, sem)
            self.to_partner(block)

    def step6(self):
        self.got(self.full.at[pl.ds(0, 16 * self.rows)], 1)
        self.got(self.part(0, 0), 2)

    def finish(self):
        self.got(self.full.at[pl.ds(0, 31 * self.rows)], 0)

    def step(self, n):
        getattr(self, "step%d" % n)()


WEIGHT_SEMS = 19


class Spread:
    def __init__(self, buf, rows, sems, pos):
        self.buf, self.rows, self.sems, self.pos = buf, rows, sems, pos
        y, x, z, c = pos
        self.starts = (((c * 4 + z) * 4 + x) * 4 + y, ((c * 4 + z) * 4 + x) * 4, (c * 4 + z) * 16, c * 64)
        self.copies = {}

    def send(self, stage):
        axis, many = ((0, 1), (1, 4), (2, 16), (3, 64))[stage]
        part = self.buf.at[pl.ds(pl.multiple_of(self.starts[stage] * self.rows, 8), many * self.rows)]
        for k in (1,) if axis == 3 else (1, 2, 3):
            at = stage * 3 + k - 1
            copy = pltpu.make_async_remote_copy(
                src_ref=part,
                dst_ref=part,
                send_sem=self.sems.at[at],
                recv_sem=self.sems.at[10 + at],
                device_id=moved(self.pos, axis, k),
                device_id_type=MESH,
            )
            copy.start()
            self.copies.setdefault(stage, []).append(copy)

    def wait(self, stage):
        for copy in self.copies[stage]:
            copy.wait()


SPREAD_SEMS = 20


def exchange(pos, axis, sems, at, source, slots):
    copies = []
    for k in (1,) if axis == 3 else (1, 2, 3):
        copies.append(
            pltpu.make_async_remote_copy(
                src_ref=source(k),
                dst_ref=slots(k),
                send_sem=sems.at[at + k - 1],
                recv_sem=sems.at[at + 2 + k],
                device_id=moved(pos, axis, k),
                device_id_type=MESH,
            )
        )
    for copy in copies:
        copy.start()
    return copies


class RowSums:
    def __init__(self, part, total, from_core, from_axis, sems, pos):
        self.part, self.total, self.from_core, self.from_axis = part, total, from_core, from_axis
        self.sems, self.pos, self.copies = sems, pos, None
        y, x, z, c = pos
        self.half = pl.multiple_of(c * 64, 16)
        self.mine = pl.multiple_of(c * 64 + z * 16, 16)

    def send(self, stage):
        y, x, z, c = self.pos
        part, total = self.part, self.total
        if stage == 0:
            other = pl.ds(pl.multiple_of((1 - c) * 64, 16), 64)
            self.copies = exchange(self.pos, 3, self.sems, 0, lambda k: part.at[other], lambda k: self.from_core)
        if stage == 1:
            at = lambda k: part.at[pl.ds(pl.multiple_of(c * 64 + lax.rem(z + k, 4) * 16, 16), 16)]
            self.copies = exchange(self.pos, 2, self.sems, 6, at, lambda k: self.from_axis.at[0, k - 1])
        if stage in (2, 3):
            at = lambda k: part.at[pl.ds(self.mine, 16)] if stage == 2 else self.from_axis.at[3, 0]
            self.copies = exchange(
                self.pos, 3 - stage, self.sems, 6 * stage, at, lambda k: self.from_axis.at[stage - 1, k - 1]
            )
        if stage == 4:
            rows = lambda k: total.at[pl.ds(self.mine, 16)]
            self.copies = exchange(self.pos, 2, self.sems, 24, rows, rows)
        if stage == 5:
            rows = lambda k: total.at[pl.ds(self.half, 64)]
            self.copies = exchange(self.pos, 3, self.sems, 30, rows, rows)

    def wait(self, stage):
        for copy in self.copies:
            copy.wait()
        slots = self.from_axis
        if stage == 0:
            self.part[pl.ds(self.half, 64)] += self.from_core[...]
        if stage in (1, 2, 3):
            mine = slots[3, 0] if stage == 3 else self.part[pl.ds(self.mine, 16)]
            out = mine + slots[stage - 1, 0] + slots[stage - 1, 1] + slots[stage - 1, 2]
            if stage == 1:
                self.part[pl.ds(self.mine, 16)] = out
            if stage == 2:
                slots[3, 0] = out
            if stage == 3:
                self.total[pl.ds(self.mine, 16)] = out


SUMS_SEMS = 36


def normalized(values):
    center = jnp.mean(values, axis=-1, keepdims=True)
    shifted = values - center
    spread = jnp.mean(shifted * shifted, axis=-1, keepdims=True)
    return shifted * lax.rsqrt(spread + epsilon)


def two_parts(values):
    high = values.astype(jnp.bfloat16)
    return high, (values - high.astype(jnp.float32)).astype(jnp.bfloat16)


def split_dot(left, right):
    high, low = two_parts(right)
    return jnp.dot(left, high, preferred_element_type=jnp.float32) + jnp.dot(
        left, low, preferred_element_type=jnp.float32
    )


def gelu(v):
    return 0.5 * v * (1.0 + lax.erf(v * 0.7071067811865476))


def named_by(codes, column, base, rows, odd):
    wanted = (base + lax.broadcasted_iota(jnp.int32, (1, rows), 1)) * 2 + odd
    first, second = codes[:, column : column + 1], codes[:, column + 1 : column + 2]
    return (first == wanted).astype(jnp.float32) + (second == wanted).astype(jnp.float32)


def encoder(
    hidden,
    gain1,
    gain2,
    gain3,
    named,
    own_qkv,
    own_out,
    own_up,
    own_down,
    table,
    pooled_out,
    sums_out,
    codes_out,
    full_qkv,
    full_out,
    full_up,
    full_down,
    hid,
    norm,
    qkv,
    mixed,
    resid,
    act,
    final,
    named_all,
    pooled_all,
    pooled_f32,
    rows_table,
    part,
    from_core,
    from_axis,
    weight_sems,
    named_sems,
    pooled_sems,
    sums_sems,
    local_sem,
):
    pos = here()
    y, x, z, c = pos
    images, seq, width = hidden.shape
    me = ((y * 4 + x) * 4 + z) * 2 + c
    place = ((c * 4 + z) * 4 + x) * 4 + y
    load_table = pltpu.make_async_copy(table, rows_table, local_sem)
    load_table.start()
    barrier = pltpu.get_barrier_semaphore()
    peers = [moved(pos, axis, k) for axis in (0, 1, 2) for k in (1, 2, 3)] + [moved(pos, 3, 1)]
    for peer in peers:
        pl.semaphore_signal(barrier, inc=1, device_id=peer, device_id_type=MESH)
    named_all[pl.ds(pl.multiple_of(place * 8, 8), 8)] = named[...]
    pl.semaphore_wait(barrier, len(peers))

    A, B, C, D = (
        Weights(own, full, weight_sems.at[n], pos)
        for n, (own, full) in enumerate(
            ((own_qkv, full_qkv), (own_out, full_out), (own_up, full_up), (own_down, full_down))
        )
    )
    ids = Spread(named_all, 8, named_sems, pos)
    pools = Spread(pooled_all, 16, pooled_sems, pos)
    sums = RowSums(part, sums_out, from_core, from_axis, sums_sems, pos)

    ids.send(0)
    A.step(0)

    def load_rows(b, at, size):
        values = hidden[b, pl.ds(at, size), :].astype(jnp.float32)
        dst = pl.ds(pl.multiple_of(b * PAD + at, 16), size)
        norm[dst] = (normalized(values) * gain1[...]).astype(jnp.bfloat16)
        hid[dst] = values.astype(jnp.bfloat16)

    for b in range(images):
        lax.fori_loop(0, seq // BLK, lambda t, _: load_rows(b, pl.multiple_of(t * BLK, BLK), BLK), None)
        last = hidden[b, seq - 1 : seq, :].astype(jnp.float32)
        keep = lax.broadcasted_iota(jnp.int32, (16, 1), 0) == 0
        rows = jnp.where(keep, jnp.broadcast_to(last, (16, width)), 0.0)
        dst = pl.ds(b * PAD + seq - 1, 16)
        norm[dst] = (normalized(rows) * gain1[...]).astype(jnp.bfloat16)
        hid[dst] = rows.astype(jnp.bfloat16)
        if b == 0:
            ids.wait(0)
            ids.send(1)
            A.step(1)

    ids.wait(1)
    ids.send(2)
    A.step(2)
    B.step(0)
    ids.wait(2)
    ids.send(3)
    A.step(3)
    B.step(1)
    ids.wait(3)

    code = named_all[pl.ds(0, 128, stride=8), :] - me * 4096
    mine = (code >= 0) & (code < 4096)
    first = jnp.max(jnp.where(mine, code, -1), axis=1, keepdims=True)
    second = jnp.min(jnp.where(mine, code, 4096), axis=1, keepdims=True)
    many = jnp.sum(mine.astype(jnp.float32), axis=1, keepdims=True)
    second = jnp.where(many > 1.5, second, -1)
    lane = lax.broadcasted_iota(jnp.int32, (128, 128), 1)
    codes_out[...] = jnp.where(lane == 0, first, jnp.where(lane == 1, second, -1))
    A.step(4)
    B.step(2)
    load_table.wait()
    part[...] = jnp.zeros_like(part)

    def row_sums(n, _):
        codes = codes_out[...]
        high, low = two_parts(rows_table[pl.ds(pl.multiple_of(n * 256, 256), 256)])
        for b in range(2):
            hits = named_by(codes, 0, n * 256, 256, b).astype(jnp.bfloat16)
            part[:, 256 * b : 256 * b + 256] += jnp.dot(hits, high, preferred_element_type=jnp.float32) + jnp.dot(
                hits, low, preferred_element_type=jnp.float32
            )

    lax.fori_loop(0, 8, row_sums, None)
    sums.send(0)
    C.step(0)
    A.step(5)
    A.step(6)

    def project(n, _):
        at = pl.ds(pl.multiple_of(n * 256, 256), 256)
        qkv[:, at] = jnp.dot(norm[...], full_qkv[:, at], preferred_element_type=jnp.float32).astype(jnp.bfloat16)

    lax.fori_loop(0, 4, project, None)
    B.step(3)
    C.step(1)
    sums.wait(0)
    sums.send(1)
    lax.fori_loop(4, 8, project, None)
    B.step(4)
    C.step(2)
    sums.wait(1)
    sums.send(2)
    lax.fori_loop(8, 12, project, None)
    B.step(5)
    sums.wait(2)
    sums.send(3)

    lower = lax.broadcasted_iota(jnp.int32, (1, 128), 1) < 64

    def attend(n, _):
        b, pair = n // 8, lax.rem(n, 8)
        top = pl.multiple_of(b * PAD, 16)
        at = [pl.ds(pl.multiple_of(pair * 128 + part_at, 128), 128) for part_at in (0, width, 2 * width)]
        query = qkv[pl.ds(top, PAD), at[0]]
        keys = qkv[pl.ds(top, 256), at[1]]
        values = qkv[pl.ds(top, 256), at[2]]
        last = pl.ds(pl.multiple_of(top + 256, 16), 16)
        last_key = qkv[last, at[1]].astype(jnp.float32)[0:1]
        last_value = qkv[last, at[2]].astype(jnp.float32)[0:1]
        with_last = query.astype(jnp.float32) * last_key
        outs = []
        for side in (lower, jnp.logical_not(lower)):
            chosen = jnp.where(side, query.astype(jnp.float32) * 0.125, 0.0).astype(jnp.bfloat16)
            scores = lax.dot_general(chosen, keys, (((1,), (1,)), ((), ())), preferred_element_type=jnp.float32)
            extra = jnp.sum(jnp.where(side, with_last, 0.0), axis=-1, keepdims=True) * 0.125
            top_score = jnp.maximum(jnp.max(scores, axis=-1, keepdims=True), extra)
            probs = jnp.exp(scores - top_score)
            extra = jnp.exp(extra - top_score)
            share = 1.0 / (jnp.sum(probs, axis=-1, keepdims=True) + extra)
            out = jnp.dot(probs.astype(jnp.bfloat16), values, preferred_element_type=jnp.float32)
            outs.append((out + extra * last_value) * share)
        mixed[pl.ds(top, PAD), at[0]] = jnp.where(lower, outs[0], outs[1]).astype(jnp.bfloat16)

    lax.fori_loop(0, 4, attend, None)
    C.step(3)
    B.step(6)
    sums.wait(3)
    sums.send(4)
    lax.fori_loop(4, 8, attend, None)
    C.step(4)
    D.step(0)
    sums.wait(4)
    sums.send(5)
    lax.fori_loop(8, 12, attend, None)
    C.step(5)
    D.step(1)
    sums.wait(5)
    lax.fori_loop(12, 16, attend, None)
    D.step(2)

    def out_project(n, _):
        at = pl.ds(pl.multiple_of(n * 256, 256), 256)
        add = jnp.dot(mixed[...], full_out[:, at], preferred_element_type=jnp.float32)
        resid[:, at] = (hid[:, at].astype(jnp.float32) + add).astype(jnp.bfloat16)

    lax.fori_loop(0, 4, out_project, None)

    def second_norm(n, _):
        at = pl.ds(pl.multiple_of(n * BLK, BLK), BLK)
        norm[at] = (normalized(resid[at].astype(jnp.float32)) * gain2[...]).astype(jnp.bfloat16)

    lax.fori_loop(0, 2 * PAD // BLK, second_norm, None)
    C.step(6)
    D.step(3)

    def up_project(n, _):
        at = pl.ds(pl.multiple_of(n * 256, 256), 256)
        act[:, at] = gelu(jnp.dot(norm[...], full_up[:, at], preferred_element_type=jnp.float32)).astype(jnp.bfloat16)

    lax.fori_loop(0, 5, up_project, None)
    D.step(4)
    lax.fori_loop(5, 10, up_project, None)
    D.step(5)
    lax.fori_loop(10, 16, up_project, None)
    D.step(6)

    def down_project(n, _):
        at = pl.ds(pl.multiple_of(n * 256, 256), 256)
        add = jnp.dot(act[...], full_down[:, at], preferred_element_type=jnp.float32)
        final[:, at] = resid[:, at].astype(jnp.float32) + add

    lax.fori_loop(0, 4, down_project, None)

    pieces = []
    for b in range(images):

        def pool(t, total):
            rows = normalized(final[pl.ds(pl.multiple_of(b * PAD + t * BLK, 16), BLK)])
            return total + jnp.sum(rows.reshape(BLK // 8, 8, width), axis=0)

        total = lax.fori_loop(0, seq // BLK, pool, jnp.zeros((8, width), jnp.float32))
        rows = normalized(final[pl.ds(b * PAD + seq - 1, 8)])
        keep = lax.broadcasted_iota(jnp.int32, (8, 1), 0) == 0
        total = jnp.sum(total + jnp.where(keep, rows, 0.0), axis=0, keepdims=True) * gain3[...] * (1.0 / seq)
        pieces.extend(total[:, 128 * n : 128 * n + 128] for n in range(width // 128))
    pooled_all[pl.ds(pl.multiple_of(place * 16, 16), 16)] = jnp.concatenate(pieces, axis=0).astype(jnp.bfloat16)
    for stage in range(4):
        pools.send(stage)
        pools.wait(stage)
    pooled_f32[...] = pooled_all[...].astype(jnp.float32)
    for b in range(2):
        for n in range(8):
            rows = pooled_f32[pl.ds(b * 8 + n, 128, stride=16), :]
            pooled_out[128 * b : 128 * b + 128, 128 * n : 128 * n + 128] = rows.astype(jnp.bfloat16)
    for weight in (A, B, C, D):
        weight.finish()


def encode(hidden, gain1, gain2, gain3, named, own, table):
    images, seq, width = hidden.shape
    rows = 2 * PAD
    sizes = [(w.shape[0] * 32, w.shape[1]) for w in own]
    bf16, f32 = jnp.bfloat16, jnp.float32
    vmem = pl.BlockSpec(memory_space=pltpu.VMEM)
    anywhere = pl.BlockSpec(memory_space=pl.ANY)
    return pl.pallas_call(
        encoder,
        out_shape=(
            jax.ShapeDtypeStruct((256, width), bf16),
            jax.ShapeDtypeStruct((128, 512), f32),
            jax.ShapeDtypeStruct((128, 128), jnp.int32),
        ),
        in_specs=[vmem] * 5 + [anywhere] * 5,
        out_specs=(vmem,) * 3,
        scratch_shapes=[pltpu.VMEM(s, bf16) for s in sizes]
        + [
            pltpu.VMEM((rows, width), bf16),
            pltpu.VMEM((rows, width), bf16),
            pltpu.VMEM((rows, 3 * width), bf16),
            pltpu.VMEM((rows, width), bf16),
            pltpu.VMEM((rows, width), bf16),
            pltpu.VMEM((rows, 4 * width), bf16),
            pltpu.VMEM((rows, width), f32),
            pltpu.VMEM((1024, 128), jnp.int32),
            pltpu.VMEM((2048, 128), bf16),
            pltpu.VMEM((2048, 128), f32),
            pltpu.VMEM(table.shape, f32),
            pltpu.VMEM((128, 512), f32),
            pltpu.VMEM((64, 512), f32),
            pltpu.VMEM((4, 3, 16, 512), f32),
            pltpu.SemaphoreType.DMA((4, WEIGHT_SEMS)),
            pltpu.SemaphoreType.DMA((SPREAD_SEMS,)),
            pltpu.SemaphoreType.DMA((SPREAD_SEMS,)),
            pltpu.SemaphoreType.DMA((SUMS_SEMS,)),
            pltpu.SemaphoreType.DMA,
        ],
        compiler_params=pltpu.CompilerParams(
            collective_id=0, has_side_effects=True, vmem_limit_bytes=58 * 1024 * 1024
        ),
        name="encoder",
    )(hidden, gain1, gain2, gain3, named, *own, table)


def align(pooled, w_proj, sums, codes, table, accum, table_new, accum_new, content_grad, proj_grad, unit, grads, columns):
    step = pl.program_id(0)

    @pl.when(step == 0)
    def _():
        y, x, z, c = here()
        me = ((y * 4 + x) * 4 + z) * 2 + c
        place = ((c * 4 + z) * 4 + x) * 4 + y
        content = jnp.dot(pooled[...], w_proj[...], preferred_element_type=jnp.float32)
        scale = lax.rsqrt(jnp.mean(content * content, axis=-1, keepdims=True) + epsilon)
        units = content * scale
        unit[...] = units
        both = jnp.concatenate([sums[:, 0:256], sums[:, 256:512]], axis=0)
        grad_unit = LOOK_IMG * units - both
        inner = jnp.mean(grad_unit * units, axis=-1, keepdims=True)
        grads[...] = scale * (grad_unit - units * inner)
        content_grad[0:1] = grads[pl.ds(place, 1)]
        content_grad[1:2] = grads[pl.ds(place + 128, 1)]
        lanes = pl.ds(pl.multiple_of(me // 16 * 128, 128), 128)
        high, low = two_parts(grads[...])
        turned = lambda right: lax.dot_general(
            pooled[:, lanes], right, (((0,), (0,)), ((), ())), preferred_element_type=jnp.float32
        )
        columns[...] = turned(high) + turned(low)
        proj_grad[...] = columns[pl.ds(pl.multiple_of(lax.rem(me, 16) * 8, 8), 8)]

    rows = table.shape[0]
    base = step * rows
    pairs = codes[...]
    hits = jnp.concatenate([named_by(pairs, 0, base, rows, b) for b in range(2)], axis=0)
    named = lax.dot_general(
        hits.astype(jnp.bfloat16),
        jnp.ones((256, 128), jnp.bfloat16),
        (((0,), (0,)), ((), ())),
        preferred_element_type=jnp.float32,
    )[:, 0:1]
    high, low = two_parts(unit[...])
    turned = lambda right: lax.dot_general(
        hits.astype(jnp.bfloat16), right, (((0,), (0,)), ((), ())), preferred_element_type=jnp.float32
    )
    grad_rows = named * table[...] - (turned(high) + turned(low))
    fresh = accum[...] + grad_rows * grad_rows
    accum_new[...] = fresh
    table_new[...] = table[...] - learn_rate * grad_rows / jnp.sqrt(fresh)


def finish(pooled, w_proj, sums, codes, table, accum):
    n, width = table.shape
    rows = 512
    whole = lambda a: pl.BlockSpec(a.shape, lambda i: (0, 0))
    tiles = pl.BlockSpec((rows, width), lambda i: (i, 0))
    f32 = jnp.float32
    return pl.pallas_call(
        align,
        grid=(n // rows,),
        out_shape=(
            jax.ShapeDtypeStruct(table.shape, f32),
            jax.ShapeDtypeStruct(table.shape, f32),
            jax.ShapeDtypeStruct((2, 256), f32),
            jax.ShapeDtypeStruct((8, 256), f32),
        ),
        in_specs=[whole(pooled), whole(w_proj), whole(sums), whole(codes), tiles, tiles],
        out_specs=(
            tiles,
            tiles,
            pl.BlockSpec((2, 256), lambda i: (0, 0)),
            pl.BlockSpec((8, 256), lambda i: (0, 0)),
        ),
        scratch_shapes=[pltpu.VMEM((256, 256), f32), pltpu.VMEM((256, 256), f32), pltpu.VMEM((128, 256), f32)],
        compiler_params=pltpu.CompilerParams(dimension_semantics=("arbitrary",)),
        name="align",
    )(pooled, w_proj, sums, codes, table, accum)


def on_device(
    hidden,
    ln1_gain,
    w_qkv,
    w_out,
    ln2_gain,
    w_up,
    w_down,
    post_gain,
    w_proj,
    table,
    accum,
    place,
    lookup_table,
    lookup_row,
):
    images = hidden.shape[0]
    rows_dev = table.shape[1]
    table_ids = jnp.arange(place.shape[0], dtype=jnp.int32)
    owners = jnp.sum(jnp.where(lookup_table == table_ids[None, :], place[None, :], 0), axis=1)
    image = jnp.arange(lookup_row.shape[0], dtype=jnp.int32) // LOOK_IMG
    named = (owners * rows_dev + lookup_row) * images + image
    named = jnp.broadcast_to(named[None, :], (8, named.shape[0]))
    pooled, sums, codes = encode(
        hidden,
        ln1_gain[None, :],
        ln2_gain[None, :],
        post_gain[None, :],
        named,
        (w_qkv, w_out, w_up, w_down),
        table[0],
    )
    table_new, accum_new, content_grad, proj_grad = finish(pooled, w_proj, sums, codes, table[0], accum[0])
    return (table_new[None], accum_new[None], content_grad, proj_grad)


def solution(mesh):
    torus = Mesh(
        mesh.devices.reshape(mesh.shape["grp"], 4, 4, 2), ("grp", "fsdp_0", "fsdp_1", "fsdp_2")
    )
    in_specs = (
        P(GRP_FSDP, None, None),
        P(),
        P(FSDP, None),
        P(FSDP, None),
        P(),
        P(FSDP, None),
        P(FSDP, None),
        P(),
        P(),
        P(GRP_FSDP, None, None),
        P(GRP_FSDP, None, None),
        P(),
        P(GRP_FSDP, None),
        P(GRP_FSDP),
    )
    out_specs = (
        P(GRP_FSDP, None, None),
        P(GRP_FSDP, None, None),
        P(GRP_FSDP, None),
        P(GRP_FSDP, None),
    )
    return jax.shard_map(
        on_device, mesh=torus, in_specs=in_specs, out_specs=out_specs, check_vma=False
    )
```

```python
import functools

import jax
import jax.numpy as jnp
from jax import lax
from jax.experimental import pallas as pl
from jax.experimental.pallas import tpu as pltpu
from jax.sharding import Mesh
from jax.sharding import PartitionSpec as P

HEADS = 16
LOOK_IMG = 64
FSDP = ("fsdp_0", "fsdp_1", "fsdp_2")
GRP_FSDP = ("grp", "fsdp_0", "fsdp_1", "fsdp_2")
MESH = pl.DeviceIdType.MESH
PAD = 272
BLK = 32

epsilon = 1e-06
learn_rate = 0.5


def here():
    return tuple(lax.axis_index(a) for a in GRP_FSDP)


def moved(pos, axis, step):
    out = list(pos)
    out[axis] = lax.rem(pos[axis] + step, 2 if axis == 3 else 4)
    return tuple(out)


def wait_bytes(ref, sem):
    pltpu.make_async_copy(ref, ref, sem).wait()


class Weights:
    def __init__(self, own, full, sems, pos):
        self.own, self.full, self.sems = own, full, sems
        y, x, z, c = pos
        self.rows = own[0].shape[0]
        self.partner = (y, x, z, 1 - c)
        d = 1 - c
        self.i, self.j, self.c = x * d + z * c, z * d + x * c, c
        self.s1, self.s2 = 8 - 6 * c, 2 + 6 * c
        self.first = {k: (y, lax.rem(x + k * d, 4), lax.rem(z + k * c, 4), c) for k in (1, 3)}
        self.second = {k: (y, lax.rem(x + k * c, 4), lax.rem(z + k * d, 4), c) for k in (1, 3)}

    def span(self, start, size):
        if len(self.full.shape) == 3:
            return self.full.at[:, pl.ds(start, size)]
        return self.full.at[pl.ds(start, size)]

    def part(self, di, dj, lo=0, size=None):
        size = self.rows if size is None else size
        block = lax.rem(self.i + di, 4) * self.s1 + lax.rem(self.j + dj, 4) * self.s2 + self.c
        return self.span(pl.multiple_of(block * self.rows + lo, 16), size)

    def fetch(self):
        mine = self.part(0, 0)
        for n, own in enumerate(self.own):
            to = mine.at[n] if len(self.own) > 1 else mine
            pltpu.make_async_copy(own, to, self.sems.at[2]).start()

    def send(self, ref, sem, device):
        pltpu.make_async_remote_copy(
            src_ref=ref,
            dst_ref=ref,
            send_sem=self.sems.at[19 if sem == 1 else 0],
            recv_sem=self.sems.at[sem],
            device_id=device,
            device_id_type=MESH,
        ).start()

    def got(self, ref, sem):
        wait_bytes(ref, self.sems.at[sem])

    def to_partner(self, ref):
        self.send(ref, 1, self.partner)

    def start(self):
        mine = self.part(0, 0)
        self.got(mine, 2)
        self.send(mine, 3, self.first[1])
        self.send(mine, 4, self.first[3])
        self.to_partner(mine)

    def send_own(self):
        mine = self.part(0, 0)
        self.send(mine, 7, self.second[1])
        self.send(mine, 11, self.second[3])

    def spread(self, di, k):
        block = self.part(di, 0)
        self.send(block, 7 + k, self.second[1])
        self.send(block, 11 + k, self.second[3])
        self.to_partner(block)

    def from_before(self):
        half = self.rows // 2
        self.got(self.part(3, 0), 3)
        self.send(self.part(3, 0, 0, half), 5, self.first[1])
        self.spread(3, 1)

    def from_after(self):
        half = self.rows // 2
        self.got(self.part(1, 0), 4)
        self.send(self.part(1, 0, half, half), 6, self.first[3])
        self.spread(1, 2)

    def opposite(self):
        half = self.rows // 2
        self.got(self.part(2, 0, 0, half), 5)
        self.got(self.part(2, 0, half, half), 6)
        self.spread(2, 3)

    def column_before(self, k):
        block = self.part(ORDER[k], 3)
        self.got(block, 7 + k)
        if k in (0, 2):
            self.send(block, 15 + k // 2, self.second[1])
        self.to_partner(block)

    def column_after(self, k):
        block = self.part(ORDER[k], 1)
        self.got(block, 11 + k)
        if k in (1, 3):
            self.send(block, 17 + k // 2, self.second[3])
        self.to_partner(block)

    def column_opposite(self, k):
        block = self.part(ORDER[k], 2)
        self.got(block, (15, 17, 16, 18)[k])
        self.to_partner(block)

    def complete(self):
        self.got(self.span(0, 16 * self.rows), 1)

    def finish(self):
        self.got(self.span(0, 16 * self.rows), 19)
        self.got(self.span(0, 15 * self.rows), 0)

    def step(self, *names):
        named = {"start": self.start, "own": self.send_own, "f-": self.from_before, "f+": self.from_after}
        named.update({"h": self.opposite, "end": self.complete})
        grouped = {"b": self.column_before, "a": self.column_after, "o": self.column_opposite, "y": self.across_step}
        for name in names:
            if name in named:
                named[name]()
            else:
                grouped[name[0]](name[1] if name[0] == "y" else int(name[1]))

    def across_step(self, name):
        raise NotImplementedError


ORDER = (0, 3, 1, 2)
WEIGHT_SEMS = 20


class Quarters(Weights):
    def __init__(self, own, full, sems, more, pos):
        y, x, z, c = pos
        rows = full.shape[3]
        super().__init__((own.at[pl.ds(pl.multiple_of(y * rows, 16), rows)],), full, sems, pos)
        self.y, self.more = y, more
        self.t1, self.t2 = 4 - 3 * c, 1 + 3 * c
        self.up, self.down = moved(pos, 0, 1), moved(pos, 0, 3)

    def part(self, di, dj, lo=0, size=None):
        size = self.rows if size is None else size
        block = lax.rem(self.i + di, 4) * self.t1 + lax.rem(self.j + dj, 4) * self.t2
        return self.full.at[block, self.c, self.y, pl.ds(lo, size)]

    def quarter(self, dy):
        return self.full.at[:, self.c, lax.rem(self.y + dy, 4)]

    def half(self, dy, lo):
        return self.full.at[pl.ds(lo, 8), self.c, lax.rem(self.y + dy, 4)]

    def across(self, ref, sem, device):
        pltpu.make_async_remote_copy(
            src_ref=ref,
            dst_ref=ref,
            send_sem=self.more.at[sem],
            recv_sem=self.more.at[7 + sem],
            device_id=device,
            device_id_type=MESH,
        ).start()

    def across_step(self, name):
        if name == "0":
            self.across(self.quarter(0), 0, self.up)
            self.across(self.quarter(0), 1, self.down)
        if name == "-":
            wait_bytes(self.quarter(3), self.more.at[7])
            self.across(self.half(3, 0), 2, self.up)
            self.across(self.quarter(3), 4, self.partner)
        if name == "+":
            wait_bytes(self.quarter(1), self.more.at[8])
            self.across(self.half(1, 8), 3, self.down)
            self.across(self.quarter(1), 5, self.partner)
        if name == "2":
            wait_bytes(self.half(2, 0), self.more.at[9])
            wait_bytes(self.half(2, 8), self.more.at[10])
            self.across(self.quarter(2), 6, self.partner)

    def complete(self):
        self.got(self.full.at[:, 0, 0], 1)
        for sem in (4, 5, 6):
            wait_bytes(self.quarter(0), self.more.at[7 + sem])

    def finish(self):
        self.got(self.full.at[:, 0, 0], 19)
        self.got(self.full.at[pl.ds(0, 15), 0, 0], 0)
        for sem in (0, 1, 4, 5, 6):
            wait_bytes(self.quarter(0), self.more.at[sem])
        for sem in (2, 3):
            wait_bytes(self.half(0, 0), self.more.at[sem])


QUARTER_SEMS = 14


class Spread:
    def __init__(self, buf, rows, sems, pos):
        self.buf, self.rows, self.sems, self.pos = buf, rows, sems, pos
        y, x, z, c = pos
        self.starts = (((c * 4 + z) * 4 + x) * 4 + y, ((c * 4 + z) * 4 + x) * 4, (c * 4 + z) * 16, c * 64)
        self.copies = {}

    def send(self, stage):
        axis, many = ((0, 1), (1, 4), (2, 16), (3, 64))[stage]
        part = self.buf.at[pl.ds(pl.multiple_of(self.starts[stage] * self.rows, 8), many * self.rows)]
        for k in (1,) if axis == 3 else (1, 2, 3):
            at = stage * 3 + k - 1
            copy = pltpu.make_async_remote_copy(
                src_ref=part,
                dst_ref=part,
                send_sem=self.sems.at[at],
                recv_sem=self.sems.at[10 + at],
                device_id=moved(self.pos, axis, k),
                device_id_type=MESH,
            )
            copy.start()
            self.copies.setdefault(stage, []).append(copy)

    def wait(self, stage):
        for copy in self.copies[stage]:
            copy.wait()


SPREAD_SEMS = 20


def exchange(pos, axis, sems, at, source, slots):
    copies = []
    for k in (1,) if axis == 3 else (1, 2, 3):
        copies.append(
            pltpu.make_async_remote_copy(
                src_ref=source(k),
                dst_ref=slots(k),
                send_sem=sems.at[at + k - 1],
                recv_sem=sems.at[at + 2 + k],
                device_id=moved(pos, axis, k),
                device_id_type=MESH,
            )
        )
    for copy in copies:
        copy.start()
    return copies


class RowSums:
    def __init__(self, part, total, from_core, from_axis, sems, pos):
        self.part, self.total, self.from_core, self.from_axis = part, total, from_core, from_axis
        self.sems, self.pos, self.copies = sems, pos, None
        y, x, z, c = pos
        self.half = pl.multiple_of(c * 64, 16)
        self.mine = pl.multiple_of(c * 64 + z * 16, 16)

    def send(self, stage):
        y, x, z, c = self.pos
        part, total = self.part, self.total
        if stage == 0:
            other = pl.ds(pl.multiple_of((1 - c) * 64, 16), 64)
            self.copies = exchange(self.pos, 3, self.sems, 0, lambda k: part.at[other], lambda k: self.from_core)
        if stage == 1:
            at = lambda k: part.at[pl.ds(pl.multiple_of(c * 64 + lax.rem(z + k, 4) * 16, 16), 16)]
            self.copies = exchange(self.pos, 2, self.sems, 6, at, lambda k: self.from_axis.at[0, k - 1])
        if stage in (2, 3):
            at = lambda k: part.at[pl.ds(self.mine, 16)] if stage == 2 else self.from_axis.at[3, 0]
            self.copies = exchange(
                self.pos, 3 - stage, self.sems, 6 * stage, at, lambda k: self.from_axis.at[stage - 1, k - 1]
            )
        if stage == 4:
            rows = lambda k: total.at[pl.ds(self.mine, 16)]
            self.copies = exchange(self.pos, 2, self.sems, 24, rows, rows)
        if stage == 5:
            rows = lambda k: total.at[pl.ds(self.half, 64)]
            self.copies = exchange(self.pos, 3, self.sems, 30, rows, rows)

    def wait(self, stage):
        for copy in self.copies:
            copy.wait()
        slots = self.from_axis
        if stage == 0:
            self.part[pl.ds(self.half, 64)] += self.from_core[...]
        if stage in (1, 2, 3):
            mine = slots[3, 0] if stage == 3 else self.part[pl.ds(self.mine, 16)]
            out = mine + slots[stage - 1, 0] + slots[stage - 1, 1] + slots[stage - 1, 2]
            if stage == 1:
                self.part[pl.ds(self.mine, 16)] = out
            if stage == 2:
                slots[3, 0] = out
            if stage == 3:
                self.total[pl.ds(self.mine, 16)] = out


SUMS_SEMS = 36


def normalized(values):
    center = jnp.mean(values, axis=-1, keepdims=True)
    shifted = values - center
    spread = jnp.mean(shifted * shifted, axis=-1, keepdims=True)
    return shifted * lax.rsqrt(spread + epsilon)


def two_parts(values):
    high = values.astype(jnp.bfloat16)
    return high, (values - high.astype(jnp.float32)).astype(jnp.bfloat16)


def split_dot(left, right):
    high, low = two_parts(right)
    return jnp.dot(left, high, preferred_element_type=jnp.float32) + jnp.dot(
        left, low, preferred_element_type=jnp.float32
    )


def gelu(v):
    return 0.5 * v * (1.0 + lax.erf(v * 0.7071067811865476))


def named_by(codes, column, base, rows, odd):
    wanted = (base + lax.broadcasted_iota(jnp.int32, (1, rows), 1)) * 2 + odd
    first, second = codes[:, column : column + 1], codes[:, column + 1 : column + 2]
    return (first == wanted).astype(jnp.float32) + (second == wanted).astype(jnp.float32)


def encoder(
    hidden,
    gain1,
    gain2,
    gain3,
    tables,
    table_rows,
    places,
    own_qkv,
    own_out,
    own_up,
    own_down,
    table,
    pooled_out,
    sums_out,
    codes_out,
    full_qkv1,
    full_qkv2,
    full_out,
    full_up1,
    full_up2,
    full_down,
    hid,
    norm,
    qkv,
    mixed,
    resid,
    act,
    final,
    named_all,
    pooled_all,
    pooled_f32,
    rows_table,
    part,
    from_core,
    from_axis,
    weight_sems,
    quarter_sems,
    named_sems,
    pooled_sems,
    sums_sems,
    local_sem,
):
    pos = here()
    y, x, z, c = pos
    seq, images, width = hidden.shape
    me = ((y * 4 + x) * 4 + z) * 2 + c
    me_place = ((c * 4 + z) * 4 + x) * 4 + y
    third = lambda half: [own_qkv.at[:, pl.ds(n * width + half * (width // 2), width // 2)] for n in range(3)]
    A1, A2, B, C1, C2 = (
        Weights(own, full, weight_sems.at[n], pos)
        for n, (own, full) in enumerate(
            (
                (third(0), full_qkv1),
                (third(1), full_qkv2),
                ([own_out], full_out),
                ([own_up.at[:, pl.ds(0, 2 * width)]], full_up1),
                ([own_up.at[:, pl.ds(2 * width, 2 * width)]], full_up2),
            )
        )
    )
    D = Quarters(own_down, full_down, weight_sems.at[5], quarter_sems, pos)
    for weight in (D, A1, A2, B, C1, C2):
        weight.fetch()
    load_table = pltpu.make_async_copy(table, rows_table, local_sem)
    load_table.start()
    barrier = pltpu.get_barrier_semaphore()
    peers = [moved(pos, axis, k) for axis in (0, 1, 2) for k in (1, 2, 3)] + [moved(pos, 3, 1)]
    for peer in peers:
        pl.semaphore_signal(barrier, inc=1, device_id=peer, device_id_type=MESH)
    down_rows = lax.broadcasted_iota(jnp.int32, (128, 128), 0)
    along = lax.broadcasted_iota(jnp.int32, (128, 128), 1)
    turned_place = jnp.sum(jnp.where(down_rows == along, places[...], 0).astype(jnp.float32), axis=1, keepdims=True)
    owners = jnp.sum(jnp.where(down_rows == tables[...], turned_place, 0.0), axis=0, keepdims=True)
    image = along[0:1] // LOOK_IMG
    named = (owners.astype(jnp.int32) * 2048 + table_rows[...]) * 2 + image
    named_all[pl.ds(pl.multiple_of(me_place * 8, 8), 8)] = jnp.broadcast_to(named, (8, 128))
    pl.semaphore_wait(barrier, len(peers))

    ids = Spread(named_all, 8, named_sems, pos)
    pools = Spread(pooled_all, 16, pooled_sems, pos)
    sums = RowSums(part, sums_out, from_core, from_axis, sums_sems, pos)

    def load_rows(b, at, size):
        values = hidden[pl.ds(at, size), b, :].astype(jnp.float32)
        dst = pl.ds(pl.multiple_of(b * PAD + at, 16), size)
        norm[dst] = (normalized(values) * gain1[...]).astype(jnp.bfloat16)
        hid[dst] = values.astype(jnp.bfloat16)

    def load(b, start, end):
        lax.fori_loop(start, end, lambda t, _: load_rows(b, pl.multiple_of(t * BLK, BLK), BLK), None)
        if end < seq // BLK:
            return
        last = hidden[seq - 1 : seq, b, :].astype(jnp.float32)
        keep = lax.broadcasted_iota(jnp.int32, (16, 1), 0) == 0
        rows = jnp.where(keep, jnp.broadcast_to(last, (16, width)), 0.0)
        dst = pl.ds(b * PAD + seq - 1, 16)
        norm[dst] = (normalized(rows) * gain1[...]).astype(jnp.bfloat16)
        hid[dst] = rows.astype(jnp.bfloat16)

    def name_rows():
        code = named_all[pl.ds(0, 128, stride=8), :] - me * 4096
        mine = (code >= 0) & (code < 4096)
        first = jnp.max(jnp.where(mine, code, -1), axis=1, keepdims=True)
        second = jnp.min(jnp.where(mine, code, 4096), axis=1, keepdims=True)
        many = jnp.sum(mine.astype(jnp.float32), axis=1, keepdims=True)
        second = jnp.where(many > 1.5, second, -1)
        lane = lax.broadcasted_iota(jnp.int32, (128, 128), 1)
        codes = jnp.where(lane == 0, first, jnp.where(lane == 1, second, -1))
        in_rows = [
            jnp.sum(jnp.where(down_rows == along, v, 0).astype(jnp.float32), axis=0, keepdims=True) for v in (first, second)
        ]
        codes_out[...] = jnp.concatenate(in_rows + [jnp.zeros((6, 128), jnp.float32)], axis=0).astype(jnp.int32)
        load_table.wait()
        part[...] = jnp.zeros_like(part)

        def row_sums(n, _):
            high, low = two_parts(rows_table[pl.ds(pl.multiple_of(n * 256, 256), 256)])
            for b in range(2):
                hits = named_by(codes, 0, n * 256, 256, b).astype(jnp.bfloat16)
                part[:, 256 * b : 256 * b + 256] += jnp.dot(hits, high, preferred_element_type=jnp.float32) + jnp.dot(
                    hits, low, preferred_element_type=jnp.float32
                )

        lax.fori_loop(0, 8, row_sums, None)

    def project(half, n, _):
        third, tile = n // 2, lax.rem(n, 2) * 256
        weight = (full_qkv1, full_qkv2)[half][third, :, pl.ds(pl.multiple_of(tile, 256), 256)]
        at = pl.ds(pl.multiple_of(third * width + half * (width // 2) + tile, 256), 256)
        qkv[:, at] = jnp.dot(norm[...], weight, preferred_element_type=jnp.float32).astype(jnp.bfloat16)

    lower = lax.broadcasted_iota(jnp.int32, (1, 128), 1) < 64

    def attend(half, n, _):
        b, pair = n // 4, half * 4 + lax.rem(n, 4)
        top = pl.multiple_of(b * PAD, 16)
        at = [pl.ds(pl.multiple_of(pair * 128 + part_at, 128), 128) for part_at in (0, width, 2 * width)]
        query = qkv[pl.ds(top, PAD), at[0]]
        keys = qkv[pl.ds(top, 256), at[1]]
        values = qkv[pl.ds(top, 256), at[2]]
        last = pl.ds(pl.multiple_of(top + 256, 16), 16)
        last_key = qkv[last, at[1]].astype(jnp.float32)[0:1]
        last_value = qkv[last, at[2]].astype(jnp.float32)[0:1]
        with_last = query.astype(jnp.float32) * last_key
        outs = []
        for side in (lower, jnp.logical_not(lower)):
            chosen = jnp.where(side, query.astype(jnp.float32) * 0.125, 0.0).astype(jnp.bfloat16)
            scores = lax.dot_general(chosen, keys, (((1,), (1,)), ((), ())), preferred_element_type=jnp.float32)
            extra = jnp.sum(jnp.where(side, with_last, 0.0), axis=-1, keepdims=True) * 0.125
            top_score = jnp.maximum(jnp.max(scores, axis=-1, keepdims=True), extra)
            probs = jnp.exp(scores - top_score)
            extra = jnp.exp(extra - top_score)
            share = 1.0 / (jnp.sum(probs, axis=-1, keepdims=True) + extra)
            out = jnp.dot(probs.astype(jnp.bfloat16), values, preferred_element_type=jnp.float32)
            outs.append((out + extra * last_value) * share)
        mixed[pl.ds(top, PAD), at[0]] = jnp.where(lower, outs[0], outs[1]).astype(jnp.bfloat16)

    def out_project(n, _):
        at = pl.ds(pl.multiple_of(n * 256, 256), 256)
        add = jnp.dot(mixed[...], full_out[:, at], preferred_element_type=jnp.float32)
        resid[:, at] = (hid[:, at].astype(jnp.float32) + add).astype(jnp.bfloat16)

    def second_norm(n, _):
        at = pl.ds(pl.multiple_of(n * BLK, BLK), BLK)
        norm[at] = (normalized(resid[at].astype(jnp.float32)) * gain2[...]).astype(jnp.bfloat16)

    def up_project(piece, n, _):
        here_at = pl.ds(pl.multiple_of(n * 256, 256), 256)
        at = pl.ds(pl.multiple_of(piece * 2 * width + n * 256, 256), 256)
        up = jnp.dot(norm[...], (full_up1, full_up2)[piece][:, here_at], preferred_element_type=jnp.float32)
        act[:, at] = gelu(up).astype(jnp.bfloat16)

    def down_project(piece, n, _):
        at = pl.ds(pl.multiple_of(n * 256, 256), 256)
        weight = full_down[pl.ds(piece * 8, 8), :, :, :, at].reshape(2 * width, 256)
        before = resid[:, at].astype(jnp.float32) if piece == 0 else final[:, at]
        left = act[:, pl.ds(piece * 2 * width, 2 * width)]
        final[:, at] = before + jnp.dot(left, weight, preferred_element_type=jnp.float32)

    run = lambda body, start, end: lax.fori_loop(start, end, body, None)

    D.step("start")
    A1.step("start")
    D.step("own")
    A1.step("own")
    ids.send(0)
    load(0, 0, 8)
    D.step("f-", "f+")
    load(1, 0, 4)
    D.step("b0", "a0")
    load(1, 4, 8)
    A1.step("f-")
    D.step("h")
    A1.step("f+")
    D.step("b1", "a1")
    A1.step("b0", "a0")
    D.step("b2", "a2", "o0")
    ids.wait(0)
    ids.send(1)
    A1.step("h", "b1", "a1")
    D.step("b3", "a3")
    A1.step("b2", "a2")
    D.step("o1")
    A1.step("o0")
    D.step("o2")
    A1.step("a3")
    A2.step("start", "own")
    A1.step("b3", "o1")
    D.step("o3", "y0")
    A1.step("o2", "o3")
    A2.step("f-", "f+", "b0")
    ids.wait(1)
    A2.step("a0")
    ids.send(2)
    A1.step("end")
    run(functools.partial(project, 0), 0, 4)
    A2.step("h", "b1", "a1")
    run(functools.partial(project, 0), 4, 6)
    A2.step("b2", "a2")
    run(functools.partial(attend, 0), 0, 2)
    A2.step("o0")
    B.step("start")
    C1.step("start")
    A2.step("b3", "a3")
    B.step("own")
    C1.step("own")
    A2.step("o1")
    run(functools.partial(attend, 0), 2, 4)
    A2.step("o2")
    run(functools.partial(attend, 0), 4, 6)
    B.step("f-", "f+", "b0")
    ids.wait(2)
    A2.step("o3")
    ids.send(3)
    run(functools.partial(attend, 0), 6, 8)
    B.step("a0")
    C1.step("f-", "f+")
    B.step("h")
    C1.step("b0")
    B.step("b1")
    A2.step("end")
    run(functools.partial(project, 1), 0, 2)
    B.step("a1", "b2")
    C1.step("a0")
    run(functools.partial(project, 1), 2, 4)
    C2.step("start")
    B.step("a2", "o0")
    C1.step("h")
    C2.step("own")
    C1.step("b1")
    ids.wait(3)
    name_rows()
    B.step("b3")
    C1.step("a1", "b2", "a2")
    sums.send(0)
    run(functools.partial(project, 1), 4, 6)
    D.step("y-", "y+")
    B.step("a3", "o1")
    C1.step("o0")
    C2.step("f-")
    B.step("o2")
    C2.step("f+")
    C1.step("a3")
    sums.wait(0)
    sums.send(1)
    run(functools.partial(attend, 1), 0, 2)
    C1.step("b3")
    C2.step("a0")
    run(functools.partial(attend, 1), 2, 4)
    C2.step("h")
    C1.step("o1")
    C2.step("b0")
    run(functools.partial(attend, 1), 4, 6)
    B.step("o3")
    C1.step("o2")
    run(functools.partial(attend, 1), 6, 8)
    C2.step("b1", "a1")
    B.step("end")
    run(out_project, 0, 4)
    C1.step("o3")
    C2.step("b2", "a2", "b3")
    sums.wait(1)
    run(second_norm, 0, 2 * PAD // BLK)
    C2.step("a3", "o0", "o1")
    C1.step("end")
    run(functools.partial(up_project, 0), 0, 2)
    D.step("y2")
    C2.step("o2")
    run(functools.partial(up_project, 0), 2, 6)
    C2.step("o3")
    run(functools.partial(up_project, 0), 6, 8)
    D.step("end")
    run(functools.partial(down_project, 0), 0, 4)
    C2.step("end")
    run(functools.partial(up_project, 1), 0, 8)
    run(functools.partial(down_project, 1), 0, 4)

    pieces = []
    for b in range(images):

        def pool(t, total):
            rows = normalized(final[pl.ds(pl.multiple_of(b * PAD + t * BLK, 16), BLK)])
            return total + jnp.sum(rows.reshape(BLK // 8, 8, width), axis=0)

        total = lax.fori_loop(0, seq // BLK, pool, jnp.zeros((8, width), jnp.float32))
        rows = normalized(final[pl.ds(b * PAD + seq - 1, 8)])
        keep = lax.broadcasted_iota(jnp.int32, (8, 1), 0) == 0
        total = jnp.sum(total + jnp.where(keep, rows, 0.0), axis=0, keepdims=True) * gain3[...] * (1.0 / seq)
        pieces.extend(total[:, 128 * n : 128 * n + 128] for n in range(width // 128))
    pooled_all[pl.ds(pl.multiple_of(me_place * 16, 16), 16)] = jnp.concatenate(pieces, axis=0).astype(jnp.bfloat16)
    for stage in range(4):
        pools.send(stage)
        sums.send(stage + 2)
        sums.wait(stage + 2)
        pools.wait(stage)
    pooled_f32[...] = pooled_all[...].astype(jnp.float32)
    for b in range(2):
        for n in range(8):
            rows = pooled_f32[pl.ds(b * 8 + n, 128, stride=16), :]
            pooled_out[128 * b : 128 * b + 128, 128 * n : 128 * n + 128] = rows.astype(jnp.bfloat16)
    for weight in (A1, A2, B, C1, C2, D):
        weight.finish()


def encode(hidden, gains, lookups, own, table):
    width = hidden.shape[2]
    rows = 2 * PAD
    sizes = [(3, width, width // 2)] * 2 + [(width, width)] + [(width, 2 * width)] * 2
    sizes.append((16, 2, 4, own[3].shape[0] // 4, width))
    bf16, f32 = jnp.bfloat16, jnp.float32
    vmem = pl.BlockSpec(memory_space=pltpu.VMEM)
    anywhere = pl.BlockSpec(memory_space=pl.ANY)
    return pl.pallas_call(
        encoder,
        out_shape=(
            jax.ShapeDtypeStruct((256, width), bf16),
            jax.ShapeDtypeStruct((128, 512), f32),
            jax.ShapeDtypeStruct((8, 128), jnp.int32),
        ),
        in_specs=[vmem] * 7 + [anywhere] * 5,
        out_specs=(vmem,) * 3,
        scratch_shapes=[pltpu.VMEM(s, bf16) for s in sizes]
        + [
            pltpu.VMEM((rows, width), bf16),
            pltpu.VMEM((rows, width), bf16),
            pltpu.VMEM((rows, 3 * width), bf16),
            pltpu.VMEM((rows, width), bf16),
            pltpu.VMEM((rows, width), bf16),
            pltpu.VMEM((rows, 4 * width), bf16),
            pltpu.VMEM((rows, width), f32),
            pltpu.VMEM((1024, 128), jnp.int32),
            pltpu.VMEM((2048, 128), bf16),
            pltpu.VMEM((2048, 128), f32),
            pltpu.VMEM(table.shape, f32),
            pltpu.VMEM((128, 512), f32),
            pltpu.VMEM((64, 512), f32),
            pltpu.VMEM((4, 3, 16, 512), f32),
            pltpu.SemaphoreType.DMA((6, WEIGHT_SEMS)),
            pltpu.SemaphoreType.DMA((QUARTER_SEMS,)),
            pltpu.SemaphoreType.DMA((SPREAD_SEMS,)),
            pltpu.SemaphoreType.DMA((SPREAD_SEMS,)),
            pltpu.SemaphoreType.DMA((SUMS_SEMS,)),
            pltpu.SemaphoreType.DMA,
        ],
        compiler_params=pltpu.CompilerParams(
            collective_id=0, has_side_effects=True, vmem_limit_bytes=58 * 1024 * 1024
        ),
        name="encoder",
    )(hidden, *gains, *lookups, *own, table)


def align(pooled, w_proj, sums, codes, table, accum, table_new, accum_new, content_grad, proj_grad, unit, grads, columns):
    step = pl.program_id(0)

    @pl.when(step == 0)
    def _():
        y, x, z, c = here()
        me = ((y * 4 + x) * 4 + z) * 2 + c
        place = ((c * 4 + z) * 4 + x) * 4 + y
        content = jnp.dot(pooled[...], w_proj[...], preferred_element_type=jnp.float32)
        scale = lax.rsqrt(jnp.mean(content * content, axis=-1, keepdims=True) + epsilon)
        units = content * scale
        unit[...] = units
        both = jnp.concatenate([sums[:, 0:256], sums[:, 256:512]], axis=0)
        grad_unit = LOOK_IMG * units - both
        inner = jnp.mean(grad_unit * units, axis=-1, keepdims=True)
        grads[...] = scale * (grad_unit - units * inner)
        content_grad[0:1] = grads[pl.ds(place, 1)]
        content_grad[1:2] = grads[pl.ds(place + 128, 1)]
        lanes = pl.ds(pl.multiple_of(me // 16 * 128, 128), 128)
        high, low = two_parts(grads[...])
        turned = lambda right: lax.dot_general(
            pooled[:, lanes], right, (((0,), (0,)), ((), ())), preferred_element_type=jnp.float32
        )
        columns[...] = turned(high) + turned(low)
        proj_grad[...] = columns[pl.ds(pl.multiple_of(lax.rem(me, 16) * 8, 8), 8)]

    rows = table.shape[0]
    base = step * rows
    wanted = (base + lax.broadcasted_iota(jnp.int32, (rows, 1), 0)) * 2
    hits = [
        (codes[0:1] == wanted + b).astype(jnp.float32) + (codes[1:2] == wanted + b).astype(jnp.float32) for b in range(2)
    ]
    hits = jnp.concatenate(hits, axis=1).astype(jnp.bfloat16)
    named = jnp.dot(hits, jnp.ones((256, 128), jnp.bfloat16), preferred_element_type=jnp.float32)[:, 0:1]
    grad_rows = named * table[...] - split_dot(hits, unit[...])
    fresh = accum[...] + grad_rows * grad_rows
    accum_new[...] = fresh
    table_new[...] = table[...] - learn_rate * grad_rows / jnp.sqrt(fresh)


def finish(pooled, w_proj, sums, codes, table, accum):
    n, width = table.shape
    rows = 512
    whole = lambda a: pl.BlockSpec(a.shape, lambda i: (0, 0))
    tiles = pl.BlockSpec((rows, width), lambda i: (i, 0))
    f32 = jnp.float32
    return pl.pallas_call(
        align,
        grid=(n // rows,),
        out_shape=(
            jax.ShapeDtypeStruct(table.shape, f32),
            jax.ShapeDtypeStruct(table.shape, f32),
            jax.ShapeDtypeStruct((2, 256), f32),
            jax.ShapeDtypeStruct((8, 256), f32),
        ),
        in_specs=[whole(pooled), whole(w_proj), whole(sums), whole(codes), tiles, tiles],
        out_specs=(
            tiles,
            tiles,
            pl.BlockSpec((2, 256), lambda i: (0, 0)),
            pl.BlockSpec((8, 256), lambda i: (0, 0)),
        ),
        scratch_shapes=[pltpu.VMEM((256, 256), f32), pltpu.VMEM((256, 256), f32), pltpu.VMEM((128, 256), f32)],
        compiler_params=pltpu.CompilerParams(dimension_semantics=("arbitrary",)),
        name="align",
    )(pooled, w_proj, sums, codes, table, accum)


def on_device(
    hidden,
    ln1_gain,
    w_qkv,
    w_out,
    ln2_gain,
    w_up,
    w_down,
    post_gain,
    w_proj,
    table,
    accum,
    place,
    lookup_table,
    lookup_row,
):
    pooled, sums, codes = encode(
        jnp.swapaxes(hidden, 0, 1),
        (ln1_gain[None, :], ln2_gain[None, :], post_gain[None, :]),
        (lookup_table.reshape(1, -1), lookup_row[None, :], place[None, :]),
        (w_qkv, w_out, w_up, w_down),
        table[0],
    )
    table_new, accum_new, content_grad, proj_grad = finish(pooled, w_proj, sums, codes, table[0], accum[0])
    return (table_new[None], accum_new[None], content_grad, proj_grad)


def solution(mesh):
    torus = Mesh(
        mesh.devices.reshape(mesh.shape["grp"], 4, 4, 2), ("grp", "fsdp_0", "fsdp_1", "fsdp_2")
    )
    in_specs = (
        P(GRP_FSDP, None, None),
        P(),
        P(FSDP, None),
        P(FSDP, None),
        P(),
        P(FSDP, None),
        P(FSDP, None),
        P(),
        P(),
        P(GRP_FSDP, None, None),
        P(GRP_FSDP, None, None),
        P(),
        P(GRP_FSDP, None),
        P(GRP_FSDP),
    )
    out_specs = (
        P(GRP_FSDP, None, None),
        P(GRP_FSDP, None, None),
        P(GRP_FSDP, None),
        P(GRP_FSDP, None),
    )
    return jax.shard_map(
        on_device, mesh=torus, in_specs=in_specs, out_specs=out_specs, check_vma=False
    )
```

```python
import functools

import jax
import jax.numpy as jnp
from jax import lax
from jax.experimental import pallas as pl
from jax.experimental.pallas import tpu as pltpu
from jax.sharding import Mesh
from jax.sharding import PartitionSpec as P

HEADS = 16
LOOK_IMG = 64
FSDP = ("fsdp_0", "fsdp_1", "fsdp_2")
GRP_FSDP = ("grp", "fsdp_0", "fsdp_1", "fsdp_2")
MESH = pl.DeviceIdType.MESH
PAD = 272
BLK = 32

epsilon = 1e-06
learn_rate = 0.5


def here():
    return tuple(lax.axis_index(a) for a in GRP_FSDP)


def moved(pos, axis, step):
    out = list(pos)
    out[axis] = lax.rem(pos[axis] + step, 2 if axis == 3 else 4)
    return tuple(out)


def wait_bytes(ref, sem):
    pltpu.make_async_copy(ref, ref, sem).wait()


class Weights:
    def __init__(self, own, full, sems, pos):
        self.own, self.full, self.sems = own, full, sems
        y, x, z, c = pos
        self.rows = own[0].shape[0]
        self.partner = (y, x, z, 1 - c)
        d = 1 - c
        self.i, self.j, self.c = x * d + z * c, z * d + x * c, c
        self.s1, self.s2 = 8 - 6 * c, 2 + 6 * c
        self.first = {k: (y, lax.rem(x + k * d, 4), lax.rem(z + k * c, 4), c) for k in (1, 3)}
        self.second = {k: (y, lax.rem(x + k * c, 4), lax.rem(z + k * d, 4), c) for k in (1, 3)}

    def span(self, start, size):
        if len(self.full.shape) == 3:
            return self.full.at[:, pl.ds(start, size)]
        return self.full.at[pl.ds(start, size)]

    def part(self, di, dj, lo=0, size=None):
        size = self.rows if size is None else size
        block = lax.rem(self.i + di, 4) * self.s1 + lax.rem(self.j + dj, 4) * self.s2 + self.c
        return self.span(pl.multiple_of(block * self.rows + lo, 16), size)

    def fetch(self):
        mine = self.part(0, 0)
        for n, own in enumerate(self.own):
            to = mine.at[n] if len(self.own) > 1 else mine
            pltpu.make_async_copy(own, to, self.sems.at[2]).start()

    def send(self, ref, sem, device):
        pltpu.make_async_remote_copy(
            src_ref=ref,
            dst_ref=ref,
            send_sem=self.sems.at[19 if sem == 1 else 0],
            recv_sem=self.sems.at[sem],
            device_id=device,
            device_id_type=MESH,
        ).start()

    def got(self, ref, sem):
        wait_bytes(ref, self.sems.at[sem])

    def to_partner(self, ref):
        self.send(ref, 1, self.partner)

    def start(self):
        mine = self.part(0, 0)
        self.got(mine, 2)
        self.send(mine, 3, self.first[1])
        self.send(mine, 4, self.first[3])
        self.to_partner(mine)

    def send_own(self):
        mine = self.part(0, 0)
        self.send(mine, 7, self.second[1])
        self.send(mine, 11, self.second[3])

    def spread(self, di, k):
        block = self.part(di, 0)
        self.send(block, 7 + k, self.second[1])
        self.send(block, 11 + k, self.second[3])
        self.to_partner(block)

    def from_before(self):
        half = self.rows // 2
        self.got(self.part(3, 0), 3)
        self.send(self.part(3, 0, 0, half), 5, self.first[1])
        self.spread(3, 1)

    def from_after(self):
        half = self.rows // 2
        self.got(self.part(1, 0), 4)
        self.send(self.part(1, 0, half, half), 6, self.first[3])
        self.spread(1, 2)

    def opposite(self):
        half = self.rows // 2
        self.got(self.part(2, 0, 0, half), 5)
        self.got(self.part(2, 0, half, half), 6)
        self.spread(2, 3)

    def column_before(self, k):
        block = self.part(ORDER[k], 3)
        self.got(block, 7 + k)
        if k in (0, 2):
            self.send(block, 15 + k // 2, self.second[1])
        self.to_partner(block)

    def column_after(self, k):
        block = self.part(ORDER[k], 1)
        self.got(block, 11 + k)
        if k in (1, 3):
            self.send(block, 17 + k // 2, self.second[3])
        self.to_partner(block)

    def column_opposite(self, k):
        block = self.part(ORDER[k], 2)
        self.got(block, (15, 17, 16, 18)[k])
        self.to_partner(block)

    def complete(self):
        self.got(self.span(0, 16 * self.rows), 1)

    def finish(self):
        self.got(self.span(0, 16 * self.rows), 19)
        self.got(self.span(0, 15 * self.rows), 0)

    def step(self, *names):
        named = {"start": self.start, "own": self.send_own, "f-": self.from_before, "f+": self.from_after}
        named.update({"h": self.opposite, "end": self.complete})
        grouped = {"b": self.column_before, "a": self.column_after, "o": self.column_opposite, "y": self.across_step}
        for name in names:
            if name in named:
                named[name]()
            else:
                grouped[name[0]](name[1] if name[0] == "y" else int(name[1]))

    def across_step(self, name):
        raise NotImplementedError


ORDER = (0, 3, 1, 2)
WEIGHT_SEMS = 20


class Quarters(Weights):
    def __init__(self, own, full, sems, more, pos):
        y, x, z, c = pos
        rows = full.shape[3]
        super().__init__((own.at[pl.ds(pl.multiple_of(y * rows, 16), rows)],), full, sems, pos)
        self.y, self.more = y, more
        self.t1, self.t2 = 4 - 3 * c, 1 + 3 * c
        self.up, self.down = moved(pos, 0, 1), moved(pos, 0, 3)

    def part(self, di, dj, lo=0, size=None):
        size = self.rows if size is None else size
        block = lax.rem(self.i + di, 4) * self.t1 + lax.rem(self.j + dj, 4) * self.t2
        return self.full.at[block, self.c, self.y, pl.ds(lo, size)]

    def quarter(self, dy):
        return self.full.at[:, self.c, lax.rem(self.y + dy, 4)]

    def half(self, dy, lo):
        return self.full.at[pl.ds(lo, 8), self.c, lax.rem(self.y + dy, 4)]

    def across(self, ref, sem, device):
        pltpu.make_async_remote_copy(
            src_ref=ref,
            dst_ref=ref,
            send_sem=self.more.at[sem],
            recv_sem=self.more.at[7 + sem],
            device_id=device,
            device_id_type=MESH,
        ).start()

    def across_step(self, name):
        if name == "0":
            self.across(self.quarter(0), 0, self.up)
            self.across(self.quarter(0), 1, self.down)
        if name == "-":
            wait_bytes(self.quarter(3), self.more.at[7])
            self.across(self.half(3, 0), 2, self.up)
            self.across(self.quarter(3), 4, self.partner)
        if name == "+":
            wait_bytes(self.quarter(1), self.more.at[8])
            self.across(self.half(1, 8), 3, self.down)
            self.across(self.quarter(1), 5, self.partner)
        if name == "2":
            wait_bytes(self.half(2, 0), self.more.at[9])
            wait_bytes(self.half(2, 8), self.more.at[10])
            self.across(self.quarter(2), 6, self.partner)

    def complete(self):
        self.got(self.full.at[:, 0, 0], 1)
        for sem in (4, 5, 6):
            wait_bytes(self.quarter(0), self.more.at[7 + sem])

    def finish(self):
        self.got(self.full.at[:, 0, 0], 19)
        self.got(self.full.at[pl.ds(0, 15), 0, 0], 0)
        for sem in (0, 1, 4, 5, 6):
            wait_bytes(self.quarter(0), self.more.at[sem])
        for sem in (2, 3):
            wait_bytes(self.half(0, 0), self.more.at[sem])


QUARTER_SEMS = 14


class Spread:
    def __init__(self, buf, rows, sems, pos):
        self.buf, self.rows, self.sems, self.pos = buf, rows, sems, pos
        y, x, z, c = pos
        self.starts = (((c * 4 + z) * 4 + x) * 4 + y, ((c * 4 + z) * 4 + x) * 4, (c * 4 + z) * 16, c * 64)
        self.copies = {}

    def send(self, stage):
        axis, many = ((0, 1), (1, 4), (2, 16), (3, 64))[stage]
        part = self.buf.at[pl.ds(pl.multiple_of(self.starts[stage] * self.rows, 8), many * self.rows)]
        for k in (1,) if axis == 3 else (1, 2, 3):
            at = stage * 3 + k - 1
            copy = pltpu.make_async_remote_copy(
                src_ref=part,
                dst_ref=part,
                send_sem=self.sems.at[at],
                recv_sem=self.sems.at[10 + at],
                device_id=moved(self.pos, axis, k),
                device_id_type=MESH,
            )
            copy.start()
            self.copies.setdefault(stage, []).append(copy)

    def wait(self, stage):
        for copy in self.copies[stage]:
            copy.wait()


SPREAD_SEMS = 20


def exchange(pos, axis, sems, at, source, slots):
    copies = []
    for k in (1,) if axis == 3 else (1, 2, 3):
        copies.append(
            pltpu.make_async_remote_copy(
                src_ref=source(k),
                dst_ref=slots(k),
                send_sem=sems.at[at + k - 1],
                recv_sem=sems.at[at + 2 + k],
                device_id=moved(pos, axis, k),
                device_id_type=MESH,
            )
        )
    for copy in copies:
        copy.start()
    return copies


class RowSums:
    def __init__(self, part, total, from_core, from_axis, sems, pos):
        self.part, self.total, self.from_core, self.from_axis = part, total, from_core, from_axis
        self.sems, self.pos, self.copies = sems, pos, None
        y, x, z, c = pos
        self.half = pl.multiple_of(c * 64, 16)
        self.mine = pl.multiple_of(c * 64 + z * 16, 16)

    def send(self, stage):
        y, x, z, c = self.pos
        part, total = self.part, self.total
        if stage == 0:
            other = pl.ds(pl.multiple_of((1 - c) * 64, 16), 64)
            self.copies = exchange(self.pos, 3, self.sems, 0, lambda k: part.at[other], lambda k: self.from_core)
        if stage == 1:
            at = lambda k: part.at[pl.ds(pl.multiple_of(c * 64 + lax.rem(z + k, 4) * 16, 16), 16)]
            self.copies = exchange(self.pos, 2, self.sems, 6, at, lambda k: self.from_axis.at[0, k - 1])
        if stage in (2, 3):
            at = lambda k: part.at[pl.ds(self.mine, 16)] if stage == 2 else self.from_axis.at[3, 0]
            self.copies = exchange(
                self.pos, 3 - stage, self.sems, 6 * stage, at, lambda k: self.from_axis.at[stage - 1, k - 1]
            )
        if stage == 4:
            rows = lambda k: total.at[pl.ds(self.mine, 16)]
            self.copies = exchange(self.pos, 2, self.sems, 24, rows, rows)
        if stage == 5:
            rows = lambda k: total.at[pl.ds(self.half, 64)]
            self.copies = exchange(self.pos, 3, self.sems, 30, rows, rows)

    def wait(self, stage):
        for copy in self.copies:
            copy.wait()
        slots = self.from_axis
        if stage == 0:
            self.part[pl.ds(self.half, 64)] += self.from_core[...]
        if stage in (1, 2, 3):
            mine = slots[3, 0] if stage == 3 else self.part[pl.ds(self.mine, 16)]
            out = mine + slots[stage - 1, 0] + slots[stage - 1, 1] + slots[stage - 1, 2]
            if stage == 1:
                self.part[pl.ds(self.mine, 16)] = out
            if stage == 2:
                slots[3, 0] = out
            if stage == 3:
                self.total[pl.ds(self.mine, 16)] = out


SUMS_SEMS = 36


def normalized(values):
    center = jnp.mean(values, axis=-1, keepdims=True)
    shifted = values - center
    spread = jnp.mean(shifted * shifted, axis=-1, keepdims=True)
    return shifted * lax.rsqrt(spread + epsilon)


def two_parts(values):
    high = values.astype(jnp.bfloat16)
    return high, (values - high.astype(jnp.float32)).astype(jnp.bfloat16)


def gelu(v):
    return 0.5 * v * (1.0 + lax.erf(v * 0.7071067811865476))


def named_by(codes, column, base, rows, odd):
    wanted = (base + lax.broadcasted_iota(jnp.int32, (1, rows), 1)) * 2 + odd
    first, second = codes[:, column : column + 1], codes[:, column + 1 : column + 2]
    return (first == wanted).astype(jnp.float32) + (second == wanted).astype(jnp.float32)


def encoder(
    gain1,
    gain2,
    gain3,
    tables,
    table_rows,
    places,
    hidden_in,
    proj_in,
    own_qkv,
    own_out,
    own_up,
    own_down,
    table,
    unit_high,
    unit_low,
    codes_out,
    content_grad,
    proj_grad,
    hidden,
    proj,
    total_sums,
    grads,
    columns,
    full_qkv1,
    full_qkv2,
    full_out,
    full_up1,
    full_up2,
    full_down,
    hid,
    norm,
    qkv,
    mixed,
    resid,
    act,
    final,
    named_all,
    pooled_all,
    pooled_f32,
    rows_table,
    part,
    from_core,
    from_axis,
    weight_sems,
    quarter_sems,
    named_sems,
    pooled_sems,
    sums_sems,
    local_sems,
):
    pos = here()
    y, x, z, c = pos
    seq, images, width = hidden.shape
    me = ((y * 4 + x) * 4 + z) * 2 + c
    me_place = ((c * 4 + z) * 4 + x) * 4 + y
    third = lambda half: [own_qkv.at[:, pl.ds(n * width + half * (width // 2), width // 2)] for n in range(3)]
    A1, A2, B, C1, C2 = (
        Weights(own, full, weight_sems.at[n], pos)
        for n, (own, full) in enumerate(
            (
                (third(0), full_qkv1),
                (third(1), full_qkv2),
                ([own_out], full_out),
                ([own_up.at[:, pl.ds(0, 2 * width)]], full_up1),
                ([own_up.at[:, pl.ds(2 * width, 2 * width)]], full_up2),
            )
        )
    )
    D = Quarters(own_down, full_down, weight_sems.at[5], quarter_sems, pos)
    for weight in (D, A1, A2, B, C1, C2):
        weight.fetch()
    load_hidden = pltpu.make_async_copy(hidden_in, hidden, local_sems.at[0])
    load_hidden.start()
    load_table = pltpu.make_async_copy(table, rows_table, local_sems.at[1])
    load_table.start()
    load_proj = pltpu.make_async_copy(proj_in, proj, local_sems.at[2])
    load_proj.start()
    barrier = pltpu.get_barrier_semaphore()
    peers = [moved(pos, axis, k) for axis in (0, 1, 2) for k in (1, 2, 3)] + [moved(pos, 3, 1)]
    for peer in peers:
        pl.semaphore_signal(barrier, inc=1, device_id=peer, device_id_type=MESH)
    down_rows = lax.broadcasted_iota(jnp.int32, (128, 128), 0)
    along = lax.broadcasted_iota(jnp.int32, (128, 128), 1)
    turned_place = jnp.sum(jnp.where(down_rows == along, places[...], 0).astype(jnp.float32), axis=1, keepdims=True)
    owners = jnp.sum(jnp.where(down_rows == tables[...], turned_place, 0.0), axis=0, keepdims=True)
    image = along[0:1] // LOOK_IMG
    named = (owners.astype(jnp.int32) * 2048 + table_rows[...]) * 2 + image
    named_all[pl.ds(pl.multiple_of(me_place * 8, 8), 8)] = jnp.broadcast_to(named, (8, 128))
    pl.semaphore_wait(barrier, len(peers))

    ids = Spread(named_all, 8, named_sems, pos)
    pools = Spread(pooled_all, 16, pooled_sems, pos)
    sums = RowSums(part, total_sums, from_core, from_axis, sums_sems, pos)

    def load_rows(b, at, size):
        values = hidden[pl.ds(at, size), b, :].astype(jnp.float32)
        dst = pl.ds(pl.multiple_of(b * PAD + at, 16), size)
        norm[dst] = (normalized(values) * gain1[...]).astype(jnp.bfloat16)
        hid[dst] = values.astype(jnp.bfloat16)

    def load(b, start, end):
        lax.fori_loop(start, end, lambda t, _: load_rows(b, pl.multiple_of(t * BLK, BLK), BLK), None)
        if end < seq // BLK:
            return
        last = hidden[seq - 1 : seq, b, :].astype(jnp.float32)
        keep = lax.broadcasted_iota(jnp.int32, (16, 1), 0) == 0
        rows = jnp.where(keep, jnp.broadcast_to(last, (16, width)), 0.0)
        dst = pl.ds(b * PAD + seq - 1, 16)
        norm[dst] = (normalized(rows) * gain1[...]).astype(jnp.bfloat16)
        hid[dst] = rows.astype(jnp.bfloat16)

    def name_rows():
        code = named_all[pl.ds(0, 128, stride=8), :] - me * 4096
        mine = (code >= 0) & (code < 4096)
        first = jnp.max(jnp.where(mine, code, -1), axis=1, keepdims=True)
        second = jnp.min(jnp.where(mine, code, 4096), axis=1, keepdims=True)
        many = jnp.sum(mine.astype(jnp.float32), axis=1, keepdims=True)
        second = jnp.where(many > 1.5, second, -1)
        lane = lax.broadcasted_iota(jnp.int32, (128, 128), 1)
        codes = jnp.where(lane == 0, first, jnp.where(lane == 1, second, -1))
        in_rows = [
            jnp.sum(jnp.where(down_rows == along, v, 0).astype(jnp.float32), axis=0, keepdims=True) for v in (first, second)
        ]
        codes_out[...] = jnp.concatenate(in_rows + [jnp.zeros((6, 128), jnp.float32)], axis=0).astype(jnp.int32)
        load_table.wait()
        part[...] = jnp.zeros_like(part)

        def row_sums(n, _):
            high, low = two_parts(rows_table[pl.ds(pl.multiple_of(n * 256, 256), 256)])
            for b in range(2):
                hits = named_by(codes, 0, n * 256, 256, b).astype(jnp.bfloat16)
                part[:, 256 * b : 256 * b + 256] += jnp.dot(hits, high, preferred_element_type=jnp.float32) + jnp.dot(
                    hits, low, preferred_element_type=jnp.float32
                )

        lax.fori_loop(0, 8, row_sums, None)

    def project(half, n, _):
        third, tile = n // 2, lax.rem(n, 2) * 256
        weight = (full_qkv1, full_qkv2)[half][third, :, pl.ds(pl.multiple_of(tile, 256), 256)]
        at = pl.ds(pl.multiple_of(third * width + half * (width // 2) + tile, 256), 256)
        qkv[:, at] = jnp.dot(norm[...], weight, preferred_element_type=jnp.float32).astype(jnp.bfloat16)

    lower = lax.broadcasted_iota(jnp.int32, (1, 128), 1) < 64

    def attend(half, n, _):
        b, pair = n // 4, half * 4 + lax.rem(n, 4)
        top = pl.multiple_of(b * PAD, 16)
        at = [pl.ds(pl.multiple_of(pair * 128 + part_at, 128), 128) for part_at in (0, width, 2 * width)]
        query = qkv[pl.ds(top, PAD), at[0]]
        keys = qkv[pl.ds(top, 256), at[1]]
        values = qkv[pl.ds(top, 256), at[2]]
        last = pl.ds(pl.multiple_of(top + 256, 16), 16)
        last_key = qkv[last, at[1]].astype(jnp.float32)[0:1]
        last_value = qkv[last, at[2]].astype(jnp.float32)[0:1]
        with_last = query.astype(jnp.float32) * last_key
        outs = []
        for side in (lower, jnp.logical_not(lower)):
            chosen = jnp.where(side, query.astype(jnp.float32) * 0.125, 0.0).astype(jnp.bfloat16)
            scores = lax.dot_general(chosen, keys, (((1,), (1,)), ((), ())), preferred_element_type=jnp.float32)
            extra = jnp.sum(jnp.where(side, with_last, 0.0), axis=-1, keepdims=True) * 0.125
            top_score = jnp.maximum(jnp.max(scores, axis=-1, keepdims=True), extra)
            probs = jnp.exp(scores - top_score)
            extra = jnp.exp(extra - top_score)
            share = 1.0 / (jnp.sum(probs, axis=-1, keepdims=True) + extra)
            out = jnp.dot(probs.astype(jnp.bfloat16), values, preferred_element_type=jnp.float32)
            outs.append((out + extra * last_value) * share)
        mixed[pl.ds(top, PAD), at[0]] = jnp.where(lower, outs[0], outs[1]).astype(jnp.bfloat16)

    def out_project(n, _):
        at = pl.ds(pl.multiple_of(n * 256, 256), 256)
        add = jnp.dot(mixed[...], full_out[:, at], preferred_element_type=jnp.float32)
        resid[:, at] = (hid[:, at].astype(jnp.float32) + add).astype(jnp.bfloat16)

    def second_norm(n, _):
        at = pl.ds(pl.multiple_of(n * BLK, BLK), BLK)
        norm[at] = (normalized(resid[at].astype(jnp.float32)) * gain2[...]).astype(jnp.bfloat16)

    def up_project(piece, n, _):
        here_at = pl.ds(pl.multiple_of(n * 256, 256), 256)
        at = pl.ds(pl.multiple_of(piece * 2 * width + n * 256, 256), 256)
        up = jnp.dot(norm[...], (full_up1, full_up2)[piece][:, here_at], preferred_element_type=jnp.float32)
        act[:, at] = gelu(up).astype(jnp.bfloat16)

    def down_project(piece, n, _):
        at = pl.ds(pl.multiple_of(n * 256, 256), 256)
        weight = full_down[pl.ds(piece * 8, 8), :, :, :, at].reshape(2 * width, 256)
        before = resid[:, at].astype(jnp.float32) if piece == 0 else final[:, at]
        left = act[:, pl.ds(piece * 2 * width, 2 * width)]
        final[:, at] = before + jnp.dot(left, weight, preferred_element_type=jnp.float32)

    run = lambda body, start, end: lax.fori_loop(start, end, body, None)

    D.step("start")
    A1.step("start")
    D.step("own")
    A1.step("own")
    ids.send(0)
    load_hidden.wait()
    load(0, 0, 8)
    D.step("f-", "f+")
    load(1, 0, 4)
    D.step("b0", "a0")
    load(1, 4, 8)
    A1.step("f-")
    D.step("h")
    A1.step("f+")
    D.step("b1", "a1")
    A1.step("b0", "a0")
    D.step("b2", "a2", "o0")
    ids.wait(0)
    ids.send(1)
    A1.step("h", "b1", "a1")
    D.step("b3", "a3")
    A1.step("b2", "a2")
    D.step("o1")
    A1.step("o0")
    A2.step("start")
    D.step("o2")
    A1.step("a3")
    B.step("start")
    A2.step("own")
    A1.step("b3")
    B.step("own")
    A1.step("o1")
    D.step("o3", "y0")
    A1.step("o2")
    A2.step("f-", "f+")
    A1.step("o3")
    B.step("f-")
    A2.step("b0")
    ids.wait(1)
    B.step("f+", "b0")
    ids.send(2)
    A2.step("a0")
    A1.step("end")
    run(functools.partial(project, 0), 0, 2)
    A2.step("h", "b1")
    B.step("a0")
    run(functools.partial(project, 0), 2, 4)
    A2.step("a1", "b2")
    B.step("h", "b1")
    run(functools.partial(project, 0), 4, 6)
    A2.step("a2", "o0")
    B.step("a1", "b2", "a2")
    run(functools.partial(attend, 0), 0, 2)
    C1.step("start")
    A2.step("a3", "b3")
    B.step("o0")
    C2.step("start")
    A2.step("o1")
    C1.step("own")
    C2.step("own")
    A2.step("o2")
    B.step("a3")
    run(functools.partial(attend, 0), 2, 4)
    B.step("b3", "o1")
    ids.wait(2)
    ids.send(3)
    run(functools.partial(attend, 0), 4, 6)
    A2.step("o3")
    B.step("o2")
    run(functools.partial(attend, 0), 6, 8)
    C1.step("f-", "f+", "b0")
    A2.step("end")
    run(functools.partial(project, 1), 0, 2)
    C1.step("a0")
    C2.step("f-", "f+")
    ids.wait(3)
    name_rows()
    B.step("o3")
    C1.step("h", "b1")
    C2.step("h", "b0", "a0")
    sums.send(0)
    C1.step("a1")
    run(functools.partial(project, 1), 2, 4)
    C1.step("b2", "a2")
    D.step("y-", "y+")
    C1.step("o0")
    sums.wait(0)
    sums.send(1)
    run(functools.partial(project, 1), 4, 6)
    C2.step("b1", "a1")
    run(functools.partial(attend, 1), 0, 2)
    C2.step("b2", "a2")
    run(functools.partial(attend, 1), 2, 4)
    C1.step("b3", "a3")
    run(functools.partial(attend, 1), 4, 6)
    C2.step("b3", "a3")
    run(functools.partial(attend, 1), 6, 8)
    C1.step("o1")
    C2.step("o0")
    B.step("end")
    run(out_project, 0, 4)
    C1.step("o2", "o3")
    C2.step("o1", "o2")
    run(second_norm, 0, 2 * PAD // BLK)
    C2.step("o3")
    C1.step("end")
    sums.wait(1)
    sums.send(2)
    run(functools.partial(up_project, 0), 0, 2)
    D.step("y2")
    run(functools.partial(up_project, 0), 2, 8)
    D.step("end")
    sums.wait(2)
    sums.send(3)
    run(functools.partial(down_project, 0), 0, 4)
    C2.step("end")
    sums.wait(3)
    sums.send(4)
    run(functools.partial(up_project, 1), 0, 8)
    sums.wait(4)
    sums.send(5)
    run(functools.partial(down_project, 1), 0, 4)
    sums.wait(5)

    pieces = []
    for b in range(images):

        def pool(t, total):
            rows = normalized(final[pl.ds(pl.multiple_of(b * PAD + t * BLK, 16), BLK)])
            return total + jnp.sum(rows.reshape(BLK // 8, 8, width), axis=0)

        total = lax.fori_loop(0, seq // BLK, pool, jnp.zeros((8, width), jnp.float32))
        rows = normalized(final[pl.ds(b * PAD + seq - 1, 8)])
        keep = lax.broadcasted_iota(jnp.int32, (8, 1), 0) == 0
        total = jnp.sum(total + jnp.where(keep, rows, 0.0), axis=0, keepdims=True) * gain3[...] * (1.0 / seq)
        pieces.extend(total[:, 128 * n : 128 * n + 128] for n in range(width // 128))
    pooled_all[pl.ds(pl.multiple_of(me_place * 16, 16), 16)] = jnp.concatenate(pieces, axis=0).astype(jnp.bfloat16)
    for stage in range(4):
        pools.send(stage)
        pools.wait(stage)
    pooled_f32[...] = pooled_all[...].astype(jnp.float32)
    load_proj.wait()
    lanes = me // 16
    shared = jnp.zeros((128, 256), jnp.float32)
    for b in range(2):
        content = jnp.zeros((128, 256), jnp.float32)
        for n in range(8):
            rows = pooled_f32[pl.ds(b * 8 + n, 128, stride=16), :].astype(jnp.bfloat16)
            content += jnp.dot(rows, proj[128 * n : 128 * n + 128], preferred_element_type=jnp.float32)
        scale = lax.rsqrt(jnp.mean(content * content, axis=-1, keepdims=True) + epsilon)
        unit = content * scale
        grad_unit = LOOK_IMG * unit - total_sums[:, 256 * b : 256 * b + 256]
        inner = jnp.mean(grad_unit * unit, axis=-1, keepdims=True)
        grad = scale * (grad_unit - unit * inner)
        at = pl.ds(128 * b, 128)
        unit_high[at], unit_low[at] = two_parts(unit)
        grads[at] = grad
        rows = pooled_f32[pl.ds(b * 8 + lanes, 128, stride=16), :].astype(jnp.bfloat16)
        for piece in two_parts(grad):
            shared += lax.dot_general(rows, piece, (((0,), (0,)), ((), ())), preferred_element_type=jnp.float32)
        content_grad[b : b + 1] = grads[pl.ds(me_place + 128 * b, 1)]
    columns[...] = shared
    proj_grad[...] = columns[pl.ds(pl.multiple_of(lax.rem(me, 16) * 8, 8), 8)]
    for weight in (A1, A2, B, C1, C2, D):
        weight.finish()


def encode(hidden, gains, lookups, w_proj, own, table):
    width = hidden.shape[2]
    rows = 2 * PAD
    sizes = [(3, width, width // 2)] * 2 + [(width, width)] + [(width, 2 * width)] * 2
    sizes.append((16, 2, 4, own[3].shape[0] // 4, width))
    bf16, f32 = jnp.bfloat16, jnp.float32
    vmem = pl.BlockSpec(memory_space=pltpu.VMEM)
    anywhere = pl.BlockSpec(memory_space=pl.ANY)
    return pl.pallas_call(
        encoder,
        out_shape=(
            jax.ShapeDtypeStruct((256, 256), bf16),
            jax.ShapeDtypeStruct((256, 256), bf16),
            jax.ShapeDtypeStruct((8, 128), jnp.int32),
            jax.ShapeDtypeStruct((2, 256), f32),
            jax.ShapeDtypeStruct((8, 256), f32),
        ),
        in_specs=[vmem] * 6 + [anywhere] * 7,
        out_specs=(vmem,) * 5,
        scratch_shapes=[
            pltpu.VMEM(hidden.shape, bf16),
            pltpu.VMEM(w_proj.shape, bf16),
            pltpu.VMEM((128, 512), f32),
            pltpu.VMEM((256, 256), f32),
            pltpu.VMEM((128, 256), f32),
        ]
        + [pltpu.VMEM(s, bf16) for s in sizes]
        + [
            pltpu.VMEM((rows, width), bf16),
            pltpu.VMEM((rows, width), bf16),
            pltpu.VMEM((rows, 3 * width), bf16),
            pltpu.VMEM((rows, width), bf16),
            pltpu.VMEM((rows, width), bf16),
            pltpu.VMEM((rows, 4 * width), bf16),
            pltpu.VMEM((rows, width), f32),
            pltpu.VMEM((1024, 128), jnp.int32),
            pltpu.VMEM((2048, 128), bf16),
            pltpu.VMEM((2048, 128), f32),
            pltpu.VMEM(table.shape, f32),
            pltpu.VMEM((128, 512), f32),
            pltpu.VMEM((64, 512), f32),
            pltpu.VMEM((4, 3, 16, 512), f32),
            pltpu.SemaphoreType.DMA((6, WEIGHT_SEMS)),
            pltpu.SemaphoreType.DMA((QUARTER_SEMS,)),
            pltpu.SemaphoreType.DMA((SPREAD_SEMS,)),
            pltpu.SemaphoreType.DMA((SPREAD_SEMS,)),
            pltpu.SemaphoreType.DMA((SUMS_SEMS,)),
            pltpu.SemaphoreType.DMA((3,)),
        ],
        compiler_params=pltpu.CompilerParams(
            collective_id=0, has_side_effects=True, vmem_limit_bytes=58 * 1024 * 1024
        ),
        name="encoder",
    )(*gains, *lookups, hidden, w_proj, *own, table)


def align(unit_high, unit_low, codes, content, shared, table, accum, table_new, accum_new, content_grad, proj_grad):
    step = pl.program_id(0)

    @pl.when(step == 0)
    def _():
        content_grad[...] = content[...]
        proj_grad[...] = shared[...]

    rows = table.shape[0]
    base = step * rows
    wanted = (base + lax.broadcasted_iota(jnp.int32, (rows, 1), 0)) * 2
    hits = [
        (codes[0:1] == wanted + b).astype(jnp.float32) + (codes[1:2] == wanted + b).astype(jnp.float32) for b in range(2)
    ]
    hits = jnp.concatenate(hits, axis=1).astype(jnp.bfloat16)
    named = jnp.dot(hits, jnp.ones((256, 128), jnp.bfloat16), preferred_element_type=jnp.float32)[:, 0:1]
    dot = lambda right: jnp.dot(hits, right[...], preferred_element_type=jnp.float32)
    grad_rows = named * table[...] - (dot(unit_high) + dot(unit_low))
    fresh = accum[...] + grad_rows * grad_rows
    accum_new[...] = fresh
    table_new[...] = table[...] - learn_rate * grad_rows / jnp.sqrt(fresh)


def finish(small, table, accum):
    n, width = table.shape
    rows = 1024
    whole = lambda a: pl.BlockSpec(a.shape, lambda i: (0, 0))
    tiles = pl.BlockSpec((rows, width), lambda i: (i, 0))
    f32 = jnp.float32
    return pl.pallas_call(
        align,
        grid=(n // rows,),
        out_shape=(
            jax.ShapeDtypeStruct(table.shape, f32),
            jax.ShapeDtypeStruct(table.shape, f32),
            jax.ShapeDtypeStruct((2, 256), f32),
            jax.ShapeDtypeStruct((8, 256), f32),
        ),
        in_specs=[whole(a) for a in small] + [tiles, tiles],
        out_specs=(
            tiles,
            tiles,
            pl.BlockSpec((2, 256), lambda i: (0, 0)),
            pl.BlockSpec((8, 256), lambda i: (0, 0)),
        ),
        compiler_params=pltpu.CompilerParams(dimension_semantics=("arbitrary",)),
        name="align",
    )(*small, table, accum)


def on_device(
    hidden,
    ln1_gain,
    w_qkv,
    w_out,
    ln2_gain,
    w_up,
    w_down,
    post_gain,
    w_proj,
    table,
    accum,
    place,
    lookup_table,
    lookup_row,
):
    small = encode(
        jnp.swapaxes(hidden, 0, 1),
        (ln1_gain[None, :], ln2_gain[None, :], post_gain[None, :]),
        (lookup_table.reshape(1, -1), lookup_row[None, :], place[None, :]),
        w_proj,
        (w_qkv, w_out, w_up, w_down),
        table[0],
    )
    table_new, accum_new, content_grad, proj_grad = finish(small, table[0], accum[0])
    return (table_new[None], accum_new[None], content_grad, proj_grad)


def solution(mesh):
    torus = Mesh(
        mesh.devices.reshape(mesh.shape["grp"], 4, 4, 2), ("grp", "fsdp_0", "fsdp_1", "fsdp_2")
    )
    in_specs = (
        P(GRP_FSDP, None, None),
        P(),
        P(FSDP, None),
        P(FSDP, None),
        P(),
        P(FSDP, None),
        P(FSDP, None),
        P(),
        P(),
        P(GRP_FSDP, None, None),
        P(GRP_FSDP, None, None),
        P(),
        P(GRP_FSDP, None),
        P(GRP_FSDP),
    )
    out_specs = (
        P(GRP_FSDP, None, None),
        P(GRP_FSDP, None, None),
        P(GRP_FSDP, None),
        P(GRP_FSDP, None),
    )
    return jax.shard_map(
        on_device, mesh=torus, in_specs=in_specs, out_specs=out_specs, check_vma=False
    )
```
